256 devices in a mesh: ctx: 16 (over y_hi, x, core), head: 16 (over y_lo, z).
Axes of the slice: x: 4, y: 4 (y_hi: 2, y_lo: 2; y = y_hi * 2 + y_lo), z: 8, core: 2. Of those that a mesh axis runs over, the one named last changes fastest.
Arguments:
- queries: bfloat16 [16384, 4096], P('ctx', 'head'), may hold values from -8 to 8
- keys: bfloat16 [16384, 1024], P('ctx'), may hold values from -8 to 8
- values: bfloat16 [16384, 1024], P('ctx'), may hold values from -8 to 8
- grad_out: bfloat16 [16384, 4096], P('ctx', 'head'), may hold values from -8 to 8
- block_index: int32 [16, 4], replicated, may hold values from 0 to 3
Outputs:
- grad_queries: bfloat16 [16384, 4096], P(('ctx', 'head'))
- grad_keys: bfloat16 [16384, 1024], P(('ctx', 'head'))
- grad_values: bfloat16 [16384, 1024], P(('ctx', 'head'))
The draws below stay inside these ranges and needn't reach their ends.
Inputs may be any that keep to these rules, and one draw needn't show every extreme that they name: block_index[c, l] is read only where c >= 2**l.
All inputs are finite; a program needn't handle non-finite values.
Results may differ from the reference program's by a relative error of at most 0.023.
Values may be sent and summed in bfloat16 or wider, within the bound.
No kernel may reach another device: no remote copies, remote signals or barrier semaphores. Data moves between devices by JAX's collectives and lax.ppermute only.
A program may use at most 64 MiB of HBM per device.

```python
import jax
import jax.numpy as jnp
from jax import lax

HD = 128
GROUP = 4
BLK = 256
SHARD = 1024
HQ = 32
KVH = 8
TOKENS = 16384
LEVELS = 4
N_CTX = 16


def shared_keys(key):
    drawn = jnp.clip(jax.random.normal(jax.random.fold_in(key, 11), (TOKENS, KVH * HD), jnp.float32), -8.0, 8.0)
    return drawn


def draw_keys(key, part):
    return shared_keys(key).astype(jnp.bfloat16)


def draw_queries(key, part):
    drawn = jnp.clip(jax.random.normal(jax.random.fold_in(key, 21), (TOKENS, HQ * HD), jnp.float32), -8.0, 8.0)
    return drawn.astype(jnp.bfloat16)


def set_ends(values, own_key, low, top_value):
    longest = values.shape.index(max(values.shape))
    spots = []
    for shift in (0, 1):
        where = [jax.random.randint(jax.random.fold_in(own_key, axis), (), 0, length) for axis, length in enumerate(values.shape)]
        where[longest] = (where[longest] + shift) % values.shape[longest]
        spots.append(tuple(where))
    return values.at[spots[0]].set(low).at[spots[1]].set(top_value)


def steps_of(own_key, shape, split, least, high):
    def one(position, shards_of):
        heights = jax.random.uniform(jax.random.fold_in(jax.random.fold_in(own_key, 6), position), (shards_of,), jnp.float32, least / len(split), high / len(split))
        return jnp.repeat(jnp.exp(heights), shape[position] // shards_of).reshape((-1,) + (1,) * (len(shape) - position - 1))

    level = one(*split[0])
    for cut in split[1:]:
        level = level * one(*cut)
    return level


def centred(rng, dims, scale, limit, split=(), dtype=jnp.bfloat16):
    gain = steps_of(rng, dims, split, -0.22, 0.18) if split else 1.0
    values = jax.random.normal(rng, dims, jnp.float32) * scale * gain
    return jnp.minimum(jnp.maximum(values, -limit), limit).astype(dtype)


def setup_inputs(seed: int = 0) -> dict:
    seeds = jax.random.split(jax.random.key(seed), 6)
    return {
        "queries": draw_queries(jax.random.fold_in(seeds[5], 71), 0),
        "keys": draw_keys(jax.random.fold_in(seeds[5], 71), 0),
        "values": centred(seeds[2], (TOKENS, KVH * HD), 1.0, 8.0, ((0, 16),)),
        "grad_out": centred(seeds[3], (TOKENS, HQ * HD), 1.0, 8.0, ((0, 16), (1, 16))),
        "block_index": set_ends(jax.random.randint(seeds[4], (N_CTX, LEVELS), 0, SHARD // BLK), jax.random.fold_in(seeds[4], 1), 0, (SHARD // BLK) - 1).astype(jnp.int32),
    }


def head_grads(query_group, key_group, value_group, grad_group, visible):
    softmax_scale = HD ** -0.5
    query_full = query_group.astype(jnp.float32)
    key_full = key_group.astype(jnp.float32)
    value_full = value_group.astype(jnp.float32)
    grad_full = grad_group.astype(jnp.float32)
    scores = jnp.einsum('hqd,kd->hqk', query_full, key_full) * softmax_scale
    scores = jnp.where(visible[None], scores, -jnp.inf)
    row_max = jnp.max(scores, axis=-1, keepdims=True)
    weights = jnp.exp(scores - row_max)
    probs = weights / jnp.sum(weights, axis=-1, keepdims=True)
    probs_low = probs.astype(jnp.bfloat16)
    grad_probs = jnp.einsum('hqd,kd->hqk', grad_full, value_full)
    delta = jnp.sum(probs * grad_probs, axis=-1, keepdims=True)
    scores_low = (probs * (grad_probs - delta)).astype(jnp.bfloat16)
    scores_full = scores_low.astype(jnp.float32)
    grad_query = (softmax_scale * jnp.einsum('hqk,kd->hqd', scores_full, key_full)).astype(jnp.bfloat16)
    grad_key = softmax_scale * jnp.einsum('hqk,hqd->kd', scores_full, query_full)
    grad_value = jnp.einsum('hqk,hqd->kd', probs_low.astype(jnp.float32), grad_full)
    return grad_query, grad_key, grad_value


def reference(queries, keys, values, grad_out, block_index):
    levels = N_CTX.bit_length() - 1
    query_split = queries.reshape(N_CTX, SHARD, KVH, GROUP, HD)
    grad_split = grad_out.reshape(N_CTX, SHARD, KVH, GROUP, HD)
    key_split = keys.reshape(N_CTX, SHARD, KVH, HD)
    value_split = values.reshape(N_CTX, SHARD, KVH, HD)
    key_total = jnp.zeros((N_CTX, SHARD, KVH, HD), jnp.float32)
    value_total = jnp.zeros((N_CTX, SHARD, KVH, HD), jnp.float32)
    causal = jnp.arange(SHARD)[None, :] <= jnp.arange(SHARD)[:, None]
    dq_parts = []
    for shard_idx in range(N_CTX):
        key_parts = [key_split[shard_idx]]
        value_parts = [value_split[shard_idx]]
        mask_parts = [causal]
        begins = []
        for level_num in range(levels):
            distance = 2 ** level_num
            source = max(shard_idx - distance, 0)
            block_begin = (block_index[shard_idx, level_num] * BLK).astype(jnp.int32)
            key_parts.append(lax.dynamic_slice_in_dim(key_split[source], block_begin, BLK, 0))
            value_parts.append(lax.dynamic_slice_in_dim(value_split[source], block_begin, BLK, 0))
            mask_parts.append(jnp.full((SHARD, BLK), shard_idx >= distance))
            begins.append(block_begin)
        key_all = jnp.concatenate(key_parts, axis=0)
        value_all = jnp.concatenate(value_parts, axis=0)
        visible = jnp.concatenate(mask_parts, axis=1)
        query_heads = jnp.transpose(query_split[shard_idx], (1, 2, 0, 3))
        grad_heads = jnp.transpose(grad_split[shard_idx], (1, 2, 0, 3))
        key_heads = jnp.transpose(key_all, (1, 0, 2))
        value_heads = jnp.transpose(value_all, (1, 0, 2))
        grad_query, grad_key, grad_value = lax.map(
            lambda items: head_grads(items[0], items[1], items[2], items[3], visible),
            (query_heads, key_heads, value_heads, grad_heads))
        dq_parts.append(jnp.transpose(grad_query, (2, 0, 1, 3)).reshape(SHARD, HQ * HD))
        key_rows = jnp.transpose(grad_key, (1, 0, 2))
        value_rows = jnp.transpose(grad_value, (1, 0, 2))
        key_total = key_total.at[shard_idx].add(key_rows[:SHARD])
        value_total = value_total.at[shard_idx].add(value_rows[:SHARD])
        for level_num in range(levels):
            source = max(shard_idx - 2 ** level_num, 0)
            lower = SHARD + level_num * BLK
            block_begin = begins[level_num]
            current = lax.dynamic_slice_in_dim(key_total[source], block_begin, BLK, 0)
            key_total = key_total.at[source].set(lax.dynamic_update_slice_in_dim(key_total[source], current + key_rows[lower:lower + BLK], block_begin, 0))
            current = lax.dynamic_slice_in_dim(value_total[source], block_begin, BLK, 0)
            value_total = value_total.at[source].set(lax.dynamic_update_slice_in_dim(value_total[source], current + value_rows[lower:lower + BLK], block_begin, 0))
    grad_queries = jnp.concatenate(dq_parts, axis=0)
    grad_keys = key_total.reshape(TOKENS, KVH * HD).astype(jnp.bfloat16)
    grad_values = value_total.reshape(TOKENS, KVH * HD).astype(jnp.bfloat16)
    return (grad_queries, grad_keys, grad_values)
```

```python
import jax
import jax.numpy as jnp
from jax import lax
from jax.experimental import pallas as pl
from jax.experimental.pallas import tpu as pltpu
from jax.sharding import PartitionSpec as P

HD = 128
BLK = 256
NEG = -1e30
SCALE = HD**-0.5
LOG2E = 1.4426950408889634
HBM = pl.BlockSpec(memory_space=pltpu.HBM)
VMEM = pl.BlockSpec(memory_space=pltpu.VMEM)
SMEM = pl.BlockSpec(memory_space=pltpu.SMEM)


def rotate(value, axis, steps):
    count = lax.axis_size(axis)
    return lax.ppermute(value, axis, [(source, (source + steps) % count) for source in range(count)])


def block_start(index_ref, ctx_index, level_num, ctx_count):
    target = jnp.minimum(ctx_index + 2**level_num, ctx_count - 1)
    return pl.multiple_of(index_ref[level_num, target] * BLK, BLK)


def gather_blocks(block_index, keys, values, ctx_count, levels):
    def body(index_ref, key_ref, value_ref, own_ref, *refs):
        sends, sems = refs[:levels], refs[levels]
        ctx_index = lax.axis_index("ctx")
        begin = pl.multiple_of(lax.axis_index("head") // 2 * HD, HD)
        copies = []
        for half, source in ((0, key_ref), (1, value_ref)):
            columns = slice(half * HD, (half + 1) * HD)
            for level_num in range(levels):
                start = block_start(index_ref, ctx_index, level_num, ctx_count)
                copies.append((source.at[pl.ds(start, BLK), pl.ds(begin, HD)], sends[level_num].at[:, columns]))
            copies.append((source.at[:, pl.ds(begin, HD)], own_ref.at[:, columns]))
        started = [
            pltpu.make_async_copy(source, target, sems.at[number])
            for number, (source, target) in enumerate(copies)
        ]
        for copy in started:
            copy.start()
        for copy in started:
            copy.wait()

    rows = keys.shape[0]
    return pl.pallas_call(
        body,
        out_shape=(jax.ShapeDtypeStruct((rows, 2 * HD), keys.dtype),)
        + (jax.ShapeDtypeStruct((BLK, 2 * HD), keys.dtype),) * levels,
        in_specs=[SMEM, HBM, HBM],
        out_specs=(VMEM,) * (levels + 1),
        scratch_shapes=[pltpu.SemaphoreType.DMA((2 * levels + 2,))],
        compiler_params=pltpu.CompilerParams(vmem_limit_bytes=4 << 20),
        name="gather_blocks",
    )(block_index, keys, values)


def dot(left, right):
    return jnp.dot(left, right, preferred_element_type=jnp.float32)


def attend(queries, grad_out, own, blocks):
    rows, width = queries.shape
    levels = len(blocks)
    row_tiles = rows // BLK
    factor = SCALE * LOG2E

    def body(q_ref, g_ref, own_ref, *refs):
        block_refs = refs[:levels]
        dq_ref, grad_ref = refs[levels : levels + 2]
        part_refs = refs[levels + 2 : 2 * levels + 2]
        kt_ref, acc_ref = refs[2 * levels + 2 :]
        ctx_index = lax.axis_index("ctx")

        def tile(number, half):
            columns = slice(half * HD, (half + 1) * HD)
            if number < row_tiles:
                return own_ref[number * BLK : (number + 1) * BLK, columns]
            return block_refs[number - row_tiles][:, columns]

        def spot(number):
            return slice(number * BLK, (number + 1) * BLK)

        for number in range(row_tiles + levels):
            kt_ref[:, spot(number)] = tile(number, 0).T
        key_at = lax.broadcasted_iota(jnp.int32, (BLK, BLK), 0)
        causal = key_at <= lax.broadcasted_iota(jnp.int32, (BLK, BLK), 1)
        live = [ctx_index >= 2**level_num for level_num in range(levels)]
        written = set()
        for head in range(width // HD):
            columns = slice(head * HD, (head + 1) * HD)
            for part in range(row_tiles):
                query = q_ref[spot(part), columns]
                grad = g_ref[spot(part), columns]
                query_t, grad_t = query.T, grad.T
                numbers = list(range(part + 1)) + [row_tiles + level_num for level_num in range(levels)]
                weights, grad_probs, tops, sums, products = {}, {}, {}, {}, {}
                for number in numbers:
                    scores = dot(tile(number, 0), query_t)
                    if number == part:
                        scores = jnp.where(causal, scores, NEG)
                    top = jnp.max(scores, axis=0, keepdims=True) * factor
                    shift = top
                    if number >= row_tiles:
                        shift = jnp.where(live[number - row_tiles], top, -NEG)
                        top = jnp.where(live[number - row_tiles], top, NEG)
                    weights[number] = jnp.exp2(scores * factor - shift)
                    grad_probs[number] = dot(tile(number, 1), grad_t)
                    tops[number] = top
                    sums[number] = jnp.sum(weights[number], axis=0, keepdims=True)
                    products[number] = jnp.sum(weights[number] * grad_probs[number], axis=0, keepdims=True)
                row_max = tops[numbers[0]]
                for number in numbers[1:]:
                    row_max = jnp.maximum(row_max, tops[number])
                ratios = {number: jnp.exp2(tops[number] - row_max) for number in numbers}
                inverse = 1.0 / sum(sums[number] * ratios[number] for number in numbers)
                delta = sum(products[number] * ratios[number] for number in numbers) * inverse
                dq_t = None
                for number in numbers:
                    probs = weights[number] * (ratios[number] * inverse)
                    scores_low = (probs * (grad_probs[number] - delta)).astype(jnp.bfloat16)
                    key_part = dot(scores_low, query)
                    value_part = dot(probs.astype(jnp.bfloat16), grad)
                    if number in written:
                        acc_ref[spot(number), :HD] += key_part
                        acc_ref[spot(number), HD:] += value_part
                    else:
                        written.add(number)
                        acc_ref[spot(number), :HD] = key_part
                        acc_ref[spot(number), HD:] = value_part
                    term = dot(kt_ref[:, spot(number)], scores_low)
                    dq_t = term if dq_t is None else dq_t + term
                dq_ref[spot(part), columns] = (dq_t * SCALE).T.astype(jnp.bfloat16)
        grad_ref[:, :HD] = acc_ref[:rows, :HD] * SCALE
        grad_ref[:, HD:] = acc_ref[:rows, HD:]
        for level_num in range(levels):
            at = spot(row_tiles + level_num)
            part_refs[level_num][:, :HD] = (acc_ref[at, :HD] * SCALE).astype(jnp.bfloat16)
            part_refs[level_num][:, HD:] = acc_ref[at, HD:].astype(jnp.bfloat16)

    keys = rows + levels * BLK
    return pl.pallas_call(
        body,
        out_shape=(
            jax.ShapeDtypeStruct(queries.shape, jnp.bfloat16),
            jax.ShapeDtypeStruct((rows, 2 * HD), jnp.float32),
        )
        + (jax.ShapeDtypeStruct((BLK, 2 * HD), jnp.bfloat16),) * levels,
        in_specs=[VMEM] * (3 + levels),
        out_specs=(VMEM,) * (2 + levels),
        scratch_shapes=[pltpu.VMEM((HD, keys), jnp.bfloat16), pltpu.VMEM((keys, 2 * HD), jnp.float32)],
        compiler_params=pltpu.CompilerParams(vmem_limit_bytes=48 << 20),
        cost_estimate=pl.CostEstimate(
            flops=10 * width * rows * keys, bytes_accessed=4 << 20, transcendentals=0
        ),
        name="attend",
    )(queries, grad_out, own, *blocks)


def add_returned(block_index, gradients, returned, ctx_count):
    levels = len(returned)

    def body(index_ref, grad_ref, *refs):
        out_ref, total_ref = refs[levels:]
        ctx_index = lax.axis_index("ctx")
        total_ref[...] = grad_ref[...]
        for level_num in range(levels):
            start = block_start(index_ref, ctx_index, level_num, ctx_count)
            total_ref[pl.ds(start, BLK), :] += refs[level_num][...].astype(jnp.float32)
        out_ref[...] = total_ref[...].astype(jnp.bfloat16)

    return pl.pallas_call(
        body,
        out_shape=jax.ShapeDtypeStruct(gradients.shape, jnp.bfloat16),
        in_specs=[SMEM] + [VMEM] * (levels + 1),
        out_specs=VMEM,
        scratch_shapes=[pltpu.VMEM(gradients.shape, jnp.float32)],
        compiler_params=pltpu.CompilerParams(vmem_limit_bytes=6 << 20),
        name="add_returned",
    )(block_index, gradients, *returned)


def lay_queries(gathered):
    count, token_rows, width = gathered.shape

    def body(in_ref, out_ref):
        for number in range(count):
            out_ref[:, number * width : (number + 1) * width] = in_ref[number]

    return pl.pallas_call(
        body,
        out_shape=jax.ShapeDtypeStruct((token_rows, count * width), gathered.dtype),
        in_specs=[VMEM],
        out_specs=VMEM,
        compiler_params=pltpu.CompilerParams(vmem_limit_bytes=4 << 20),
        name="lay_queries",
    )(gathered)


def lay_keys(gathered):
    count, token_rows, width = gathered.shape

    def body(in_ref, key_ref, value_ref):
        for number in range(count // 2):
            total = in_ref[2 * number].astype(jnp.float32) + in_ref[2 * number + 1].astype(jnp.float32)
            total = total.astype(jnp.bfloat16)
            key_ref[:, number * HD : (number + 1) * HD] = total[:, :HD]
            value_ref[:, number * HD : (number + 1) * HD] = total[:, HD:]

    shape = jax.ShapeDtypeStruct((token_rows, count // 2 * HD), gathered.dtype)
    return pl.pallas_call(
        body,
        out_shape=(shape, shape),
        in_specs=[VMEM],
        out_specs=(VMEM, VMEM),
        compiler_params=pltpu.CompilerParams(vmem_limit_bytes=4 << 20),
        name="lay_keys",
    )(gathered)


def spread(value, head_count):
    split = value.reshape(head_count, value.shape[0] // head_count, value.shape[1])
    return lax.all_to_all(split, "head", split_axis=0, concat_axis=0, tiled=True)


def on_device(queries, keys, values, grad_out, block_index):
    ctx_count = lax.axis_size("ctx")
    head_count = lax.axis_size("head")
    levels = ctx_count.bit_length() - 1
    block_index = block_index.T
    own, *sends = gather_blocks(block_index, keys, values, ctx_count, levels)
    blocks = [rotate(sends[level_num], "ctx", 2**level_num) for level_num in range(levels)]
    dq_local, gradients, *parts = attend(queries, grad_out, own, blocks)
    dq_gathered = spread(dq_local, head_count)
    returned = [rotate(parts[level_num], "ctx", -(2**level_num)) for level_num in range(levels)]
    summed = add_returned(block_index, gradients, returned, ctx_count)
    grad_queries = lay_queries(dq_gathered)
    grad_keys, grad_values = lay_keys(spread(summed, head_count))
    return (grad_queries, grad_keys, grad_values)


def solution(mesh):
    placed = (P("ctx", "head"), P("ctx", None), P("ctx", None), P("ctx", "head"), P())
    return jax.shard_map(
        on_device,
        mesh=mesh,
        in_specs=placed,
        out_specs=(P(("ctx", "head"), None), P(("ctx", "head"), None), P(("ctx", "head"), None)),
        check_vma=False,
    )
```

```python
import jax
import jax.numpy as jnp
from jax import lax
from jax.experimental import pallas as pl
from jax.experimental.pallas import tpu as pltpu
from jax.sharding import PartitionSpec as P

HD = 128
BLK = 256
NEG = -1e30
SCALE = HD**-0.5
FACTOR = SCALE * 1.4426950408889634
HBM = pl.BlockSpec(memory_space=pltpu.HBM)
VMEM = pl.BlockSpec(memory_space=pltpu.VMEM)
SMEM = pl.BlockSpec(memory_space=pltpu.SMEM)


def rotate(value, axis, steps):
    count = lax.axis_size(axis)
    return lax.ppermute(value, axis, [(source, (source + steps) % count) for source in range(count)])


def block_start(index_ref, ctx_index, level_num, ctx_count):
    target = jnp.minimum(ctx_index + 2**level_num, ctx_count - 1)
    return pl.multiple_of(index_ref[level_num, target] * BLK, BLK)


def gather_blocks(block_index, keys, values, ctx_count, levels):
    def body(index_ref, key_ref, value_ref, own_ref, *refs):
        sends, sems = refs[:levels], refs[levels]
        ctx_index = lax.axis_index("ctx")
        begin = pl.multiple_of(lax.axis_index("head") // 2 * HD, HD)
        copies = []
        for half, source in ((0, key_ref), (1, value_ref)):
            columns = slice(half * HD, (half + 1) * HD)
            for level_num in range(levels):
                start = block_start(index_ref, ctx_index, level_num, ctx_count)
                copies.append((source.at[pl.ds(start, BLK), pl.ds(begin, HD)], sends[level_num].at[:, columns]))
            copies.append((source.at[:, pl.ds(begin, HD)], own_ref.at[:, columns]))
        started = [
            pltpu.make_async_copy(source, target, sems.at[number])
            for number, (source, target) in enumerate(copies)
        ]
        for copy in started:
            copy.start()
        for copy in started:
            copy.wait()

    rows = keys.shape[0]
    keys = pltpu.with_memory_space_constraint(keys, pltpu.HBM)
    values = pltpu.with_memory_space_constraint(values, pltpu.HBM)
    return pl.pallas_call(
        body,
        out_shape=(jax.ShapeDtypeStruct((rows, 2 * HD), keys.dtype),)
        + (jax.ShapeDtypeStruct((BLK, 2 * HD), keys.dtype),) * levels,
        in_specs=[SMEM, HBM, HBM],
        out_specs=(VMEM,) * (levels + 1),
        scratch_shapes=[pltpu.SemaphoreType.DMA((2 * levels + 2,))],
        compiler_params=pltpu.CompilerParams(vmem_limit_bytes=4 << 20),
        name="gather_blocks",
    )(block_index, keys, values)


def dot(left, right):
    return jnp.dot(left, right, preferred_element_type=jnp.float32)


def spot(number):
    return slice(number * BLK, (number + 1) * BLK)


def params(mib):
    return pltpu.CompilerParams(vmem_limit_bytes=mib << 20)


def cost(dots, nbytes):
    return pl.CostEstimate(flops=dots * 2 * BLK * BLK * HD, bytes_accessed=nbytes, transcendentals=0)


def pairs(row_tiles):
    return [(part, number) for part in range(row_tiles) for number in range(part + 1)]


def own_scores(queries, grad_out, own):
    rows, width = queries.shape
    row_tiles, heads = rows // BLK, width // HD
    places = pairs(row_tiles)
    total = heads * len(places)

    def body(q_ref, g_ref, own_ref, weight_ref, prob_ref, stat_ref):
        key_at = lax.broadcasted_iota(jnp.int32, (BLK, BLK), 0)
        causal = key_at <= lax.broadcasted_iota(jnp.int32, (BLK, BLK), 1)
        for head in range(heads):
            columns = slice(head * HD, (head + 1) * HD)
            for part in range(row_tiles):
                query_t, grad_t = q_ref[spot(part), columns].T, g_ref[spot(part), columns].T
                for number in range(part + 1):
                    place = head * len(places) + places.index((part, number))
                    scores = dot(own_ref[spot(number), :HD], query_t)
                    if number == part:
                        scores = jnp.where(causal, scores, NEG)
                    top = jnp.max(scores, axis=0, keepdims=True) * FACTOR
                    weights = jnp.exp2(scores * FACTOR - top)
                    grad_probs = dot(own_ref[spot(number), HD:], grad_t)
                    weight_ref[place] = weights
                    prob_ref[place] = grad_probs
                    stat_ref[0, place : place + 1] = top
                    stat_ref[1, place : place + 1] = jnp.sum(weights, axis=0, keepdims=True)
                    stat_ref[2, place : place + 1] = jnp.sum(weights * grad_probs, axis=0, keepdims=True)

    tiles = jax.ShapeDtypeStruct((total, BLK, BLK), jnp.float32)
    return pl.pallas_call(
        body,
        out_shape=(tiles, tiles, jax.ShapeDtypeStruct((3, total, BLK), jnp.float32)),
        in_specs=[VMEM] * 3,
        out_specs=(VMEM,) * 3,
        compiler_params=params(16),
        cost_estimate=cost(2 * total, 2 << 20),
        name="own_scores",
    )(queries, grad_out, own)


def partner_part(queries, grad_out, blocks, stats):
    rows, width = queries.shape
    levels, row_tiles, heads = len(blocks), rows // BLK, width // HD
    places = pairs(row_tiles)
    total = heads * len(places)

    def body(q_ref, g_ref, stat_ref, *refs):
        block_refs, part_refs = refs[:levels], refs[levels : 2 * levels]
        low_ref, coef_ref, acc_ref = refs[2 * levels :]
        ctx_index = lax.axis_index("ctx")
        live = [ctx_index >= 2**level_num for level_num in range(levels)]
        for head in range(heads):
            columns = slice(head * HD, (head + 1) * HD)
            for part in range(row_tiles):
                query, grad = q_ref[spot(part), columns], g_ref[spot(part), columns]
                query_t, grad_t = query.T, grad.T
                weights, grad_probs, tops, sums, products = [], [], [], [], []
                for level_num in range(levels):
                    scores = dot(block_refs[level_num][:, :HD], query_t)
                    top = jnp.max(scores, axis=0, keepdims=True) * FACTOR
                    weight = jnp.exp2(scores * FACTOR - jnp.where(live[level_num], top, -NEG))
                    grad_prob = dot(block_refs[level_num][:, HD:], grad_t)
                    weights.append(weight)
                    grad_probs.append(grad_prob)
                    tops.append(jnp.where(live[level_num], top, NEG))
                    sums.append(jnp.sum(weight, axis=0, keepdims=True))
                    products.append(jnp.sum(weight * grad_prob, axis=0, keepdims=True))
                first = head * len(places) + places.index((part, 0))
                for place in range(first, first + part + 1):
                    tops.append(stat_ref[0, place : place + 1])
                    sums.append(stat_ref[1, place : place + 1])
                    products.append(stat_ref[2, place : place + 1])
                row_max = tops[0]
                for top in tops[1:]:
                    row_max = jnp.maximum(row_max, top)
                ratios = [jnp.exp2(top - row_max) for top in tops]
                inverse = 1.0 / sum(each * ratio for each, ratio in zip(sums, ratios))
                delta = sum(each * ratio for each, ratio in zip(products, ratios)) * inverse
                for number in range(part + 1):
                    place = first + number
                    coef_ref[place : place + 1] = ratios[levels + number] * inverse
                at = total + head * row_tiles + part
                coef_ref[at : at + 1] = delta
                for level_num in range(levels):
                    probs = weights[level_num] * (ratios[level_num] * inverse)
                    low = (probs * (grad_probs[level_num] - delta)).astype(jnp.bfloat16)
                    low_ref[head * row_tiles + part, spot(level_num)] = low
                    key_part, value_part = dot(low, query), dot(probs.astype(jnp.bfloat16), grad)
                    if head == 0 and part == 0:
                        acc_ref[spot(level_num), :HD] = key_part
                        acc_ref[spot(level_num), HD:] = value_part
                    elif head == heads - 1 and part == row_tiles - 1:
                        key_part = (acc_ref[spot(level_num), :HD] + key_part) * SCALE
                        part_refs[level_num][:, :HD] = key_part.astype(jnp.bfloat16)
                        value_part = acc_ref[spot(level_num), HD:] + value_part
                        part_refs[level_num][:, HD:] = value_part.astype(jnp.bfloat16)
                    else:
                        acc_ref[spot(level_num), :HD] += key_part
                        acc_ref[spot(level_num), HD:] += value_part

    held = total + heads * row_tiles
    return pl.pallas_call(
        body,
        out_shape=(jax.ShapeDtypeStruct((BLK, 2 * HD), jnp.bfloat16),) * levels
        + (
            jax.ShapeDtypeStruct((heads * row_tiles, levels * BLK, BLK), jnp.bfloat16),
            jax.ShapeDtypeStruct((held, BLK), jnp.float32),
        ),
        in_specs=[VMEM] * (3 + levels),
        out_specs=(VMEM,) * (2 + levels),
        scratch_shapes=[pltpu.VMEM((levels * BLK, 2 * HD), jnp.float32)],
        compiler_params=params(16),
        cost_estimate=cost(4 * heads * row_tiles * levels, 2 << 20),
        name="partner_part",
    )(queries, grad_out, stats, *blocks)


def own_part(queries, grad_out, own, blocks, weights, grad_probs, low, coef):
    rows, width = queries.shape
    levels, row_tiles, heads = len(blocks), rows // BLK, width // HD
    places = pairs(row_tiles)
    total = heads * len(places)

    def body(q_ref, g_ref, own_ref, weight_ref, prob_ref, low_ref, coef_ref, *refs):
        block_refs = refs[:levels]
        dq_ref, grad_ref, kt_ref = refs[levels:]
        for number in range(row_tiles):
            kt_ref[:, spot(number)] = own_ref[spot(number), :HD].T
        for level_num in range(levels):
            kt_ref[:, spot(row_tiles + level_num)] = block_refs[level_num][:, :HD].T
        for head in range(heads):
            columns = slice(head * HD, (head + 1) * HD)
            for part in range(row_tiles):
                query, grad = q_ref[spot(part), columns], g_ref[spot(part), columns]
                at = total + head * row_tiles + part
                delta = coef_ref[at : at + 1]
                dq_t = dot(kt_ref[:, rows:], low_ref[head * row_tiles + part])
                for number in range(part + 1):
                    place = head * len(places) + places.index((part, number))
                    probs = weight_ref[place] * coef_ref[place : place + 1]
                    scores_low = (probs * (prob_ref[place] - delta)).astype(jnp.bfloat16)
                    key_part, value_part = dot(scores_low, query), dot(probs.astype(jnp.bfloat16), grad)
                    dq_t += dot(kt_ref[:, spot(number)], scores_low)
                    if head == 0 and number == part:
                        grad_ref[spot(number), :HD] = key_part
                        grad_ref[spot(number), HD:] = value_part
                    else:
                        grad_ref[spot(number), :HD] += key_part
                        grad_ref[spot(number), HD:] += value_part
                dq_ref[spot(part), columns] = (dq_t * SCALE).T.astype(jnp.bfloat16)

    return pl.pallas_call(
        body,
        out_shape=(
            jax.ShapeDtypeStruct(queries.shape, jnp.bfloat16),
            jax.ShapeDtypeStruct((rows, 2 * HD), jnp.float32),
        ),
        in_specs=[VMEM] * (7 + levels),
        out_specs=(VMEM,) * 2,
        scratch_shapes=[pltpu.VMEM((HD, rows + levels * BLK), jnp.bfloat16)],
        compiler_params=params(16),
        cost_estimate=cost(3 * total + heads * row_tiles * levels, 2 << 20),
        name="own_part",
    )(queries, grad_out, own, weights, grad_probs, low, coef, *blocks)


def add_returned(block_index, dq_local, gradients, returned, ctx_count):
    levels, width = len(returned), dq_local.shape[1]

    def body(index_ref, dq_ref, grad_ref, *refs):
        out_ref, total_ref = refs[levels:]
        ctx_index = lax.axis_index("ctx")
        total_ref[:, :HD] = grad_ref[:, :HD] * SCALE
        total_ref[:, HD:] = grad_ref[:, HD:]
        for level_num in range(levels):
            start = block_start(index_ref, ctx_index, level_num, ctx_count)
            total_ref[pl.ds(start, BLK), :] += refs[level_num][...].astype(jnp.float32)
        out_ref[:, :width] = dq_ref[...]
        out_ref[:, width:] = total_ref[...].astype(jnp.bfloat16)

    rows = dq_local.shape[0]
    return pl.pallas_call(
        body,
        out_shape=jax.ShapeDtypeStruct((rows, width + 2 * HD), jnp.bfloat16),
        in_specs=[SMEM] + [VMEM] * (levels + 2),
        out_specs=VMEM,
        scratch_shapes=[pltpu.VMEM(gradients.shape, jnp.float32)],
        compiler_params=params(6),
        name="add_returned",
    )(block_index, dq_local, gradients, *returned)


def lay_out(gathered, width):
    count, token_rows, _ = gathered.shape

    def body(in_ref, query_ref, key_ref, value_ref):
        for number in range(count):
            query_ref[:, number * width : (number + 1) * width] = in_ref[number, :, :width]
        for number in range(count // 2):
            total = in_ref[2 * number, :, width:].astype(jnp.float32)
            total += in_ref[2 * number + 1, :, width:].astype(jnp.float32)
            total = total.astype(jnp.bfloat16)
            key_ref[:, number * HD : (number + 1) * HD] = total[:, :HD]
            value_ref[:, number * HD : (number + 1) * HD] = total[:, HD:]

    shape = jax.ShapeDtypeStruct((token_rows, count // 2 * HD), gathered.dtype)
    return pl.pallas_call(
        body,
        out_shape=(jax.ShapeDtypeStruct((token_rows, count * width), gathered.dtype), shape, shape),
        in_specs=[VMEM],
        out_specs=(VMEM,) * 3,
        compiler_params=params(6),
        name="lay_out",
    )(gathered)


def on_device(queries, keys, values, grad_out, block_index):
    ctx_count = lax.axis_size("ctx")
    head_count = lax.axis_size("head")
    levels = ctx_count.bit_length() - 1
    rows, width = queries.shape
    block_index = block_index.T
    own, *sends = gather_blocks(block_index, keys, values, ctx_count, levels)
    blocks = [rotate(sends[level_num], "ctx", 2**level_num) for level_num in range(levels)]
    weights, grad_probs, stats = own_scores(queries, grad_out, own)
    *parts, low, coef = partner_part(queries, grad_out, blocks, stats)
    returned = [rotate(parts[level_num], "ctx", -(2**level_num)) for level_num in range(levels)]
    dq_local, gradients = own_part(queries, grad_out, own, blocks, weights, grad_probs, low, coef)
    joined = add_returned(block_index, dq_local, gradients, returned, ctx_count)
    split = joined.reshape(head_count, rows // head_count, joined.shape[1])
    gathered = lax.all_to_all(split, "head", split_axis=0, concat_axis=0, tiled=True)
    return tuple(lay_out(gathered, width))


def solution(mesh):
    placed = (P("ctx", "head"), P("ctx", None), P("ctx", None), P("ctx", "head"), P())
    return jax.shard_map(
        on_device,
        mesh=mesh,
        in_specs=placed,
        out_specs=(P(("ctx", "head"), None), P(("ctx", "head"), None), P(("ctx", "head"), None)),
        check_vma=False,
    )
```

```python
import jax
import jax.numpy as jnp
from jax import lax
from jax.experimental import pallas as pl
from jax.experimental.pallas import tpu as pltpu
from jax.sharding import PartitionSpec as P

HD = 128
BLK = 256
NEG = -1e30
SCALE = HD**-0.5
FACTOR = SCALE * 1.4426950408889634
HBM = pl.BlockSpec(memory_space=pltpu.HBM)
VMEM = pl.BlockSpec(memory_space=pltpu.VMEM)
SMEM = pl.BlockSpec(memory_space=pltpu.SMEM)


def rotate(value, axis, steps):
    count = lax.axis_size(axis)
    return lax.ppermute(value, axis, [(source, (source + steps) % count) for source in range(count)])


def block_start(index_ref, ctx_index, level_num, ctx_count):
    target = jnp.minimum(ctx_index + 2**level_num, ctx_count - 1)
    return pl.multiple_of(index_ref[level_num, target] * BLK, BLK)


def send_blocks(block_index, keys, values, ctx_count, levels):
    def body(index_hbm, key_ref, value_ref, *refs):
        sends, index_ref, sems = refs[:levels], refs[levels], refs[levels + 1]
        fetch = pltpu.make_async_copy(index_hbm, index_ref, sems.at[2 * levels])
        fetch.start()
        ctx_index = lax.axis_index("ctx")
        begin = pl.multiple_of(lax.axis_index("head") // 2 * HD, HD)
        fetch.wait()
        started = []
        for level_num in range(levels):
            start = block_start(index_ref, ctx_index, level_num, ctx_count)
            for half, source in ((0, key_ref), (1, value_ref)):
                started.append(
                    pltpu.make_async_copy(
                        source.at[pl.ds(start, BLK), pl.ds(begin, HD)],
                        sends[level_num].at[:, half * HD : (half + 1) * HD],
                        sems.at[2 * level_num + half],
                    )
                )
                started[-1].start()
        for copy in started:
            copy.wait()

    return pl.pallas_call(
        body,
        out_shape=(jax.ShapeDtypeStruct((BLK, 2 * HD), keys.dtype),) * levels,
        in_specs=[HBM, HBM, HBM],
        out_specs=(VMEM,) * levels,
        scratch_shapes=[
            pltpu.SMEM(block_index.shape, jnp.int32),
            pltpu.SemaphoreType.DMA((2 * levels + 1,)),
        ],
        compiler_params=params(4),
        name="send_blocks",
    )(block_index, keys, values)


def dot(left, right):
    return jnp.dot(left, right, preferred_element_type=jnp.float32)


def spot(number):
    return slice(number * BLK, (number + 1) * BLK)


def params(mib):
    return pltpu.CompilerParams(vmem_limit_bytes=mib << 20)


def cost(dots, nbytes):
    return pl.CostEstimate(flops=dots * 2 * BLK * BLK * HD, bytes_accessed=nbytes, transcendentals=0)


def pairs(row_tiles):
    return [(part, number) for part in range(row_tiles) for number in range(part + 1)]


def score_tile(key_tile, value_tile, query_t, grad_t, seen=None):
    scores = dot(key_tile, query_t)
    if seen is not None:
        scores = jnp.where(seen, scores, NEG)
    top = jnp.max(scores, axis=0, keepdims=True) * FACTOR
    weights = jnp.exp2(scores * FACTOR - top)
    grad_probs = dot(value_tile, grad_t)
    total = jnp.sum(weights, axis=0, keepdims=True)
    product = jnp.sum(weights * grad_probs, axis=0, keepdims=True)
    return weights, grad_probs, (top, total, product)


def own_scores(queries, grad_out, keys, values):
    rows, width = queries.shape
    row_tiles, heads = rows // BLK, width // HD
    places = pairs(row_tiles)
    total = heads * len(places)

    def body(q_ref, g_ref, key_ref, value_ref, own_ref, qt_ref, gt_ref, weight_ref, prob_ref, stat_ref, sems):
        begin = pl.multiple_of(lax.axis_index("head") // 2 * HD, HD)
        started = []
        for half, source in ((0, key_ref), (1, value_ref)):
            started.append(
                pltpu.make_async_copy(
                    source.at[:, pl.ds(begin, HD)], own_ref.at[:, half * HD : (half + 1) * HD], sems.at[half]
                )
            )
            started[-1].start()
        for head in range(heads):
            columns = slice(head * HD, (head + 1) * HD)
            for part in range(row_tiles):
                qt_ref[columns, spot(part)] = q_ref[spot(part), columns].T
                gt_ref[columns, spot(part)] = g_ref[spot(part), columns].T
        for copy in started:
            copy.wait()
        key_at = lax.broadcasted_iota(jnp.int32, (BLK, BLK), 0)
        causal = key_at <= lax.broadcasted_iota(jnp.int32, (BLK, BLK), 1)
        for head in range(heads):
            columns = slice(head * HD, (head + 1) * HD)
            for part in range(row_tiles):
                query_t, grad_t = qt_ref[columns, spot(part)], gt_ref[columns, spot(part)]
                for number in range(part + 1):
                    place = head * len(places) + places.index((part, number))
                    weight_ref[place], prob_ref[place], found = score_tile(
                        own_ref[spot(number), :HD],
                        own_ref[spot(number), HD:],
                        query_t,
                        grad_t,
                        causal if number == part else None,
                    )
                    for row, each in enumerate(found):
                        stat_ref[row, place : place + 1] = each

    tiles = jax.ShapeDtypeStruct((total, BLK, BLK), jnp.float32)
    turned = jax.ShapeDtypeStruct((width, rows), jnp.bfloat16)
    return pl.pallas_call(
        body,
        out_shape=(
            jax.ShapeDtypeStruct((rows, 2 * HD), keys.dtype),
            turned,
            turned,
            tiles,
            tiles,
            jax.ShapeDtypeStruct((3, total, BLK), jnp.float32),
        ),
        in_specs=[VMEM, VMEM, HBM, HBM],
        out_specs=(VMEM,) * 6,
        scratch_shapes=[pltpu.SemaphoreType.DMA((2,))],
        compiler_params=params(8),
        cost_estimate=cost(2 * total, 2 << 20),
        name="own_scores",
    )(queries, grad_out, keys, values)


def block_scores(queries_t, grad_t, block):
    width, rows = queries_t.shape
    row_tiles, heads = rows // BLK, width // HD

    def body(qt_ref, gt_ref, block_ref, weight_ref, prob_ref, stat_ref):
        for head in range(heads):
            columns = slice(head * HD, (head + 1) * HD)
            for part in range(row_tiles):
                place = head * row_tiles + part
                weight_ref[place], prob_ref[place], found = score_tile(
                    block_ref[:, :HD], block_ref[:, HD:], qt_ref[columns, spot(part)], gt_ref[columns, spot(part)]
                )
                for row, each in enumerate(found):
                    stat_ref[row, place : place + 1] = each

    tiles = jax.ShapeDtypeStruct((heads * row_tiles, BLK, BLK), jnp.float32)
    return pl.pallas_call(
        body,
        out_shape=(tiles, tiles, jax.ShapeDtypeStruct((3, heads * row_tiles, BLK), jnp.float32)),
        in_specs=[VMEM] * 3,
        out_specs=(VMEM,) * 3,
        compiler_params=params(8),
        cost_estimate=cost(2 * heads * row_tiles, 2 << 20),
        name="block_scores",
    )(queries_t, grad_t, block)


def partner_part(queries, grad_out, own_stats, scored):
    rows, width = queries.shape
    levels, row_tiles, heads = len(scored), rows // BLK, width // HD
    places = pairs(row_tiles)
    total = heads * len(places)

    def body(q_ref, g_ref, own_ref, *refs):
        scored_refs = [refs[3 * level_num : 3 * level_num + 3] for level_num in range(levels)]
        part_refs = refs[3 * levels : 4 * levels]
        low_ref, coef_ref, acc_ref = refs[4 * levels :]
        ctx_index = lax.axis_index("ctx")
        live = [ctx_index >= 2**level_num for level_num in range(levels)]
        ratio_of = {}
        for head in range(heads):
            for part in range(row_tiles):
                at = head * row_tiles + part
                tops, sums, products = [], [], []
                for level_num in range(levels):
                    stat_ref = scored_refs[level_num][2]
                    tops.append(jnp.where(live[level_num], stat_ref[0, at : at + 1], NEG))
                    sums.append(stat_ref[1, at : at + 1])
                    products.append(stat_ref[2, at : at + 1])
                first = head * len(places) + places.index((part, 0))
                for place in range(first, first + part + 1):
                    tops.append(own_ref[0, place : place + 1])
                    sums.append(own_ref[1, place : place + 1])
                    products.append(own_ref[2, place : place + 1])
                row_max = tops[0]
                for top in tops[1:]:
                    row_max = jnp.maximum(row_max, top)
                ratios = [jnp.exp2(top - row_max) for top in tops]
                inverse = 1.0 / sum(each * ratio for each, ratio in zip(sums, ratios))
                delta = sum(each * ratio for each, ratio in zip(products, ratios)) * inverse
                for number in range(part + 1):
                    coef_ref[first + number : first + number + 1] = ratios[levels + number] * inverse
                coef_ref[total + at : total + at + 1] = delta
                ratio_of[at] = [ratio * inverse for ratio in ratios[:levels]], delta
        for level_num in range(levels):
            weight_ref, prob_ref, _ = scored_refs[level_num]
            for head in range(heads):
                columns = slice(head * HD, (head + 1) * HD)
                for part in range(row_tiles):
                    at = head * row_tiles + part
                    ratios, delta = ratio_of[at]
                    query, grad = q_ref[spot(part), columns], g_ref[spot(part), columns]
                    probs = weight_ref[at] * ratios[level_num]
                    low = (probs * (prob_ref[at] - delta)).astype(jnp.bfloat16)
                    low_ref[at, spot(level_num)] = low
                    key_part, value_part = dot(low, query), dot(probs.astype(jnp.bfloat16), grad)
                    if head == 0 and part == 0:
                        acc_ref[spot(level_num), :HD] = key_part
                        acc_ref[spot(level_num), HD:] = value_part
                    elif head == heads - 1 and part == row_tiles - 1:
                        key_part = (acc_ref[spot(level_num), :HD] + key_part) * SCALE
                        part_refs[level_num][:, :HD] = key_part.astype(jnp.bfloat16)
                        value_part = acc_ref[spot(level_num), HD:] + value_part
                        part_refs[level_num][:, HD:] = value_part.astype(jnp.bfloat16)
                    else:
                        acc_ref[spot(level_num), :HD] += key_part
                        acc_ref[spot(level_num), HD:] += value_part

    held = total + heads * row_tiles
    return pl.pallas_call(
        body,
        out_shape=(jax.ShapeDtypeStruct((BLK, 2 * HD), jnp.bfloat16),) * levels
        + (
            jax.ShapeDtypeStruct((heads * row_tiles, levels * BLK, BLK), jnp.bfloat16),
            jax.ShapeDtypeStruct((held, BLK), jnp.float32),
        ),
        in_specs=[VMEM] * (3 + 3 * levels),
        out_specs=(VMEM,) * (2 + levels),
        scratch_shapes=[pltpu.VMEM((levels * BLK, 2 * HD), jnp.float32)],
        compiler_params=params(8),
        cost_estimate=cost(2 * heads * row_tiles * levels, 2 << 20),
        name="partner_part",
    )(queries, grad_out, own_stats, *[each for level in scored for each in level])


def own_part(queries, grad_out, own, blocks, weights, grad_probs, low, coef):
    rows, width = queries.shape
    levels, row_tiles, heads = len(blocks), rows // BLK, width // HD
    places = pairs(row_tiles)
    total = heads * len(places)

    def body(q_ref, g_ref, own_ref, weight_ref, prob_ref, low_ref, coef_ref, *refs):
        block_refs = refs[:levels]
        dq_ref, grad_ref, kt_ref = refs[levels:]
        for number in range(row_tiles):
            kt_ref[:, spot(number)] = own_ref[spot(number), :HD].T
        for level_num in range(levels):
            kt_ref[:, spot(row_tiles + level_num)] = block_refs[level_num][:, :HD].T
        for head in range(heads):
            columns = slice(head * HD, (head + 1) * HD)
            for part in range(row_tiles):
                query, grad = q_ref[spot(part), columns], g_ref[spot(part), columns]
                at = total + head * row_tiles + part
                delta = coef_ref[at : at + 1]
                dq_t = dot(kt_ref[:, rows:], low_ref[head * row_tiles + part])
                for number in range(part + 1):
                    place = head * len(places) + places.index((part, number))
                    probs = weight_ref[place] * coef_ref[place : place + 1]
                    scores_low = (probs * (prob_ref[place] - delta)).astype(jnp.bfloat16)
                    key_part, value_part = dot(scores_low, query), dot(probs.astype(jnp.bfloat16), grad)
                    dq_t += dot(kt_ref[:, spot(number)], scores_low)
                    if head == 0 and number == part:
                        grad_ref[spot(number), :HD] = key_part
                        grad_ref[spot(number), HD:] = value_part
                    else:
                        grad_ref[spot(number), :HD] += key_part
                        grad_ref[spot(number), HD:] += value_part
                dq_ref[spot(part), columns] = (dq_t * SCALE).T.astype(jnp.bfloat16)

    return pl.pallas_call(
        body,
        out_shape=(
            jax.ShapeDtypeStruct(queries.shape, jnp.bfloat16),
            jax.ShapeDtypeStruct((rows, 2 * HD), jnp.float32),
        ),
        in_specs=[VMEM] * (7 + levels),
        out_specs=(VMEM,) * 2,
        scratch_shapes=[pltpu.VMEM((HD, rows + levels * BLK), jnp.bfloat16)],
        compiler_params=params(8),
        cost_estimate=cost(3 * total + heads * row_tiles * levels, 2 << 20),
        name="own_part",
    )(queries, grad_out, own, weights, grad_probs, low, coef, *blocks)


def add_returned(block_index, dq_local, gradients, returned, ctx_count):
    levels, width = len(returned), dq_local.shape[1]

    def body(index_ref, dq_ref, grad_ref, *refs):
        out_ref, total_ref = refs[levels:]
        ctx_index = lax.axis_index("ctx")
        total_ref[:, :HD] = grad_ref[:, :HD] * SCALE
        total_ref[:, HD:] = grad_ref[:, HD:]
        for level_num in range(levels):
            start = block_start(index_ref, ctx_index, level_num, ctx_count)
            total_ref[pl.ds(start, BLK), :] += refs[level_num][...].astype(jnp.float32)
        out_ref[:, :width] = dq_ref[...]
        out_ref[:, width:] = total_ref[...].astype(jnp.bfloat16)

    rows = dq_local.shape[0]
    return pl.pallas_call(
        body,
        out_shape=jax.ShapeDtypeStruct((rows, width + 2 * HD), jnp.bfloat16),
        in_specs=[SMEM] + [VMEM] * (levels + 2),
        out_specs=VMEM,
        scratch_shapes=[pltpu.VMEM(gradients.shape, jnp.float32)],
        compiler_params=params(6),
        name="add_returned",
    )(block_index, dq_local, gradients, *returned)


def lay_out(gathered, width):
    count, token_rows, _ = gathered.shape

    def body(in_ref, query_ref, key_ref, value_ref):
        for number in range(count):
            query_ref[:, number * width : (number + 1) * width] = in_ref[number, :, :width]
        for number in range(count // 2):
            total = in_ref[2 * number, :, width:].astype(jnp.float32)
            total += in_ref[2 * number + 1, :, width:].astype(jnp.float32)
            total = total.astype(jnp.bfloat16)
            key_ref[:, number * HD : (number + 1) * HD] = total[:, :HD]
            value_ref[:, number * HD : (number + 1) * HD] = total[:, HD:]

    shape = jax.ShapeDtypeStruct((token_rows, count // 2 * HD), gathered.dtype)
    return pl.pallas_call(
        body,
        out_shape=(jax.ShapeDtypeStruct((token_rows, count * width), gathered.dtype), shape, shape),
        in_specs=[VMEM],
        out_specs=(VMEM,) * 3,
        compiler_params=params(6),
        name="lay_out",
    )(gathered)


def on_device(queries, keys, values, grad_out, block_index):
    ctx_count = lax.axis_size("ctx")
    head_count = lax.axis_size("head")
    levels = ctx_count.bit_length() - 1
    rows, width = queries.shape
    block_index = block_index.T
    hbm = [pltpu.with_memory_space_constraint(each, pltpu.HBM) for each in (block_index, keys, values)]
    sends = send_blocks(*hbm, ctx_count, levels)
    blocks = [rotate(sends[level_num], "ctx", 2**level_num) for level_num in range(levels)]
    own, queries_t, grad_t, weights, grad_probs, stats = own_scores(queries, grad_out, *hbm[1:])
    scored = [block_scores(queries_t, grad_t, block) for block in blocks]
    *parts, low, coef = partner_part(queries, grad_out, stats, scored)
    returned = [rotate(parts[level_num], "ctx", -(2**level_num)) for level_num in range(levels)]
    dq_local, gradients = own_part(queries, grad_out, own, blocks, weights, grad_probs, low, coef)
    joined = add_returned(block_index, dq_local, gradients, returned, ctx_count)
    split = joined.reshape(head_count, rows // head_count, joined.shape[1])
    gathered = lax.all_to_all(split, "head", split_axis=0, concat_axis=0, tiled=True)
    return tuple(lay_out(gathered, width))


def solution(mesh):
    placed = (P("ctx", "head"), P("ctx", None), P("ctx", None), P("ctx", "head"), P())
    return jax.shard_map(
        on_device,
        mesh=mesh,
        in_specs=placed,
        out_specs=(P(("ctx", "head"), None), P(("ctx", "head"), None), P(("ctx", "head"), None)),
        check_vma=False,
    )
```

```python
import jax
import jax.numpy as jnp
from jax import lax
from jax.experimental import pallas as pl
from jax.experimental.pallas import tpu as pltpu
from jax.sharding import PartitionSpec as P

HD = 128
BLK = 256
NEG = -1e30
SCALE = HD**-0.5
FACTOR = SCALE * 1.4426950408889634
HBM = pl.BlockSpec(memory_space=pltpu.HBM)
VMEM = pl.BlockSpec(memory_space=pltpu.VMEM)
SMEM = pl.BlockSpec(memory_space=pltpu.SMEM)


def rotate(value, axis, steps):
    count = lax.axis_size(axis)
    return lax.ppermute(value, axis, [(source, (source + steps) % count) for source in range(count)])


def block_start(index_ref, ctx_index, level_num, ctx_count):
    target = jnp.minimum(ctx_index + 2**level_num, ctx_count - 1)
    return pl.multiple_of(index_ref[level_num, target] * BLK, BLK)


def gather_blocks(block_index, keys, values, ctx_count, levels):
    def body(index_hbm, key_ref, value_ref, own_ref, *refs):
        sends, index_ref, sems = refs[:levels], refs[levels], refs[levels + 1]
        begin = pl.multiple_of(lax.axis_index("head") // 2 * HD, HD)
        started = [pltpu.make_async_copy(index_hbm, index_ref, sems.at[2])]
        for half, source in ((0, key_ref), (1, value_ref)):
            started.append(
                pltpu.make_async_copy(
                    source.at[:, pl.ds(begin, HD)], own_ref.at[:, half * HD : (half + 1) * HD], sems.at[half]
                )
            )
        for copy in started:
            copy.start()
        for copy in started:
            copy.wait()
        ctx_index = lax.axis_index("ctx")
        for level_num in range(levels):
            start = block_start(index_ref, ctx_index, level_num, ctx_count)
            sends[level_num][...] = own_ref[pl.ds(start, BLK), :]

    return pl.pallas_call(
        body,
        out_shape=(jax.ShapeDtypeStruct((keys.shape[0], 2 * HD), keys.dtype),)
        + (jax.ShapeDtypeStruct((BLK, 2 * HD), keys.dtype),) * levels,
        in_specs=[HBM, HBM, HBM],
        out_specs=(VMEM,) * (levels + 1),
        scratch_shapes=[pltpu.SMEM(block_index.shape, jnp.int32), pltpu.SemaphoreType.DMA((3,))],
        compiler_params=params(4),
        name="gather_blocks",
    )(block_index, keys, values)


def dot(left, right):
    return jnp.dot(left, right, preferred_element_type=jnp.float32)


def spot(number):
    return slice(number * BLK, (number + 1) * BLK)


def params(mib):
    return pltpu.CompilerParams(vmem_limit_bytes=mib << 20)


def cost(dots, nbytes):
    return pl.CostEstimate(flops=dots * 2 * BLK * BLK * HD, bytes_accessed=nbytes, transcendentals=0)


def pairs(row_tiles):
    return [(part, number) for part in range(row_tiles) for number in range(part + 1)]


def score_tile(key_tile, value_tile, query_t, grad_t, seen=None):
    scores = dot(key_tile, query_t)
    if seen is not None:
        scores = jnp.where(seen, scores, NEG)
    top = jnp.max(scores, axis=0, keepdims=True) * FACTOR
    weights = jnp.exp2(scores * FACTOR - top)
    grad_probs = dot(value_tile, grad_t)
    total = jnp.sum(weights, axis=0, keepdims=True)
    product = jnp.sum(weights * grad_probs, axis=0, keepdims=True)
    return weights, grad_probs, (top, total, product)


def own_scores(queries, grad_out, own):
    rows, width = queries.shape
    row_tiles, heads = rows // BLK, width // HD
    places = pairs(row_tiles)
    total = heads * len(places)

    def body(q_ref, g_ref, own_ref, qt_ref, gt_ref, weight_ref, prob_ref, stat_ref):
        key_at = lax.broadcasted_iota(jnp.int32, (BLK, BLK), 0)
        causal = key_at <= lax.broadcasted_iota(jnp.int32, (BLK, BLK), 1)
        for head in range(heads):
            columns = slice(head * HD, (head + 1) * HD)
            for part in range(row_tiles):
                query_t, grad_t = q_ref[spot(part), columns].T, g_ref[spot(part), columns].T
                qt_ref[columns, spot(part)] = query_t
                gt_ref[columns, spot(part)] = grad_t
                for number in range(part + 1):
                    place = head * len(places) + places.index((part, number))
                    weight_ref[place], prob_ref[place], found = score_tile(
                        own_ref[spot(number), :HD],
                        own_ref[spot(number), HD:],
                        query_t,
                        grad_t,
                        causal if number == part else None,
                    )
                    for row, each in enumerate(found):
                        stat_ref[row, place : place + 1] = each

    tiles = jax.ShapeDtypeStruct((total, BLK, BLK), jnp.float32)
    turned = jax.ShapeDtypeStruct((width, rows), jnp.bfloat16)
    return pl.pallas_call(
        body,
        out_shape=(turned, turned, tiles, tiles, jax.ShapeDtypeStruct((3, total, BLK), jnp.float32)),
        in_specs=[VMEM] * 3,
        out_specs=(VMEM,) * 5,
        compiler_params=params(8),
        cost_estimate=cost(2 * total, 2 << 20),
        name="own_scores",
    )(queries, grad_out, own)


def block_scores(queries_t, grad_t, block):
    width, rows = queries_t.shape
    row_tiles, heads = rows // BLK, width // HD

    def body(qt_ref, gt_ref, block_ref, weight_ref, prob_ref, stat_ref):
        for head in range(heads):
            columns = slice(head * HD, (head + 1) * HD)
            for part in range(row_tiles):
                place = head * row_tiles + part
                weight_ref[place], prob_ref[place], found = score_tile(
                    block_ref[:, :HD], block_ref[:, HD:], qt_ref[columns, spot(part)], gt_ref[columns, spot(part)]
                )
                for row, each in enumerate(found):
                    stat_ref[row, place : place + 1] = each

    tiles = jax.ShapeDtypeStruct((heads * row_tiles, BLK, BLK), jnp.float32)
    return pl.pallas_call(
        body,
        out_shape=(tiles, tiles, jax.ShapeDtypeStruct((3, heads * row_tiles, BLK), jnp.float32)),
        in_specs=[VMEM] * 3,
        out_specs=(VMEM,) * 3,
        compiler_params=params(8),
        cost_estimate=cost(2 * heads * row_tiles, 2 << 20),
        name="block_scores",
    )(queries_t, grad_t, block)


def partner_part(queries, grad_out, own_stats, scored):
    rows, width = queries.shape
    levels, row_tiles, heads = len(scored), rows // BLK, width // HD
    places = pairs(row_tiles)
    total = heads * len(places)

    def body(q_ref, g_ref, own_ref, *refs):
        scored_refs = [refs[3 * level_num : 3 * level_num + 3] for level_num in range(levels)]
        part_refs = refs[3 * levels : 4 * levels]
        low_ref, coef_ref, high_ref = refs[4 * levels :]
        ctx_index = lax.axis_index("ctx")
        live = [ctx_index >= 2**level_num for level_num in range(levels)]
        ratio_of = {}
        for head in range(heads):
            for part in range(row_tiles):
                at = head * row_tiles + part
                tops, sums, products = [], [], []
                for level_num in range(levels):
                    stat_ref = scored_refs[level_num][2]
                    tops.append(jnp.where(live[level_num], stat_ref[0, at : at + 1], NEG))
                    sums.append(stat_ref[1, at : at + 1])
                    products.append(stat_ref[2, at : at + 1])
                first = head * len(places) + places.index((part, 0))
                for place in range(first, first + part + 1):
                    tops.append(own_ref[0, place : place + 1])
                    sums.append(own_ref[1, place : place + 1])
                    products.append(own_ref[2, place : place + 1])
                row_max = tops[0]
                for top in tops[1:]:
                    row_max = jnp.maximum(row_max, top)
                ratios = [jnp.exp2(top - row_max) for top in tops]
                inverse = 1.0 / sum(each * ratio for each, ratio in zip(sums, ratios))
                delta = sum(each * ratio for each, ratio in zip(products, ratios)) * inverse
                for number in range(part + 1):
                    coef_ref[first + number : first + number + 1] = ratios[levels + number] * inverse
                coef_ref[total + at : total + at + 1] = delta
                ratio_of[at] = [ratio * inverse for ratio in ratios[:levels]], delta
        for level_num in range(levels):
            weight_ref, prob_ref, _ = scored_refs[level_num]
            key_part = value_part = 0.0
            for head in range(heads):
                columns = slice(head * HD, (head + 1) * HD)
                for part in range(row_tiles):
                    at = head * row_tiles + part
                    ratios, delta = ratio_of[at]
                    probs = weight_ref[at] * ratios[level_num]
                    low = (probs * (prob_ref[at] - delta)).astype(jnp.bfloat16)
                    low_ref[head, spot(level_num), spot(part)] = low
                    high_ref[head, spot(level_num), spot(part)] = probs.astype(jnp.bfloat16)
                key_part += dot(low_ref[head, spot(level_num)], q_ref[:, columns])
                value_part += dot(high_ref[head, spot(level_num)], g_ref[:, columns])
            part_refs[level_num][:, :HD] = (key_part * SCALE).astype(jnp.bfloat16)
            part_refs[level_num][:, HD:] = value_part.astype(jnp.bfloat16)

    held = total + heads * row_tiles
    return pl.pallas_call(
        body,
        out_shape=(jax.ShapeDtypeStruct((BLK, 2 * HD), jnp.bfloat16),) * levels
        + (
            jax.ShapeDtypeStruct((heads, levels * BLK, rows), jnp.bfloat16),
            jax.ShapeDtypeStruct((held, BLK), jnp.float32),
        ),
        in_specs=[VMEM] * (3 + 3 * levels),
        out_specs=(VMEM,) * (2 + levels),
        scratch_shapes=[pltpu.VMEM((heads, levels * BLK, rows), jnp.bfloat16)],
        compiler_params=params(8),
        cost_estimate=cost(2 * heads * row_tiles * levels, 2 << 20),
        name="partner_part",
    )(queries, grad_out, own_stats, *[each for level in scored for each in level])


def own_part(queries, grad_out, own, blocks, weights, grad_probs, low, coef):
    rows, width = queries.shape
    levels, row_tiles, heads = len(blocks), rows // BLK, width // HD
    places = pairs(row_tiles)
    total = heads * len(places)

    def body(q_ref, g_ref, own_ref, weight_ref, prob_ref, low_ref, coef_ref, *refs):
        block_refs = refs[:levels]
        joined_ref, grad_ref, kt_ref, own_low_ref, high_ref = refs[levels:]
        for number in range(row_tiles):
            kt_ref[:, spot(number)] = own_ref[spot(number), :HD].T
        for level_num in range(levels):
            kt_ref[:, spot(row_tiles + level_num)] = block_refs[level_num][:, :HD].T
        for head in range(heads):
            columns = slice(head * HD, (head + 1) * HD)
            for part in range(row_tiles):
                at = total + head * row_tiles + part
                delta = coef_ref[at : at + 1]
                for number in range(part + 1):
                    place = head * len(places) + places.index((part, number))
                    probs = weight_ref[place] * coef_ref[place : place + 1]
                    low = (probs * (prob_ref[place] - delta)).astype(jnp.bfloat16)
                    own_low_ref[head, spot(number), spot(part)] = low
                    high_ref[head, spot(number), spot(part)] = probs.astype(jnp.bfloat16)
                dq_t = dot(kt_ref[:, rows:], low_ref[head, :, spot(part)])
                seen = slice(0, (part + 1) * BLK)
                dq_t += dot(kt_ref[:, seen], own_low_ref[head, seen, spot(part)])
                joined_ref[spot(part), columns] = (dq_t * SCALE).T.astype(jnp.bfloat16)
        for number in range(row_tiles):
            key_part = value_part = 0.0
            seeing = slice(number * BLK, rows)
            for head in range(heads):
                columns = slice(head * HD, (head + 1) * HD)
                key_part += dot(own_low_ref[head, spot(number), seeing], q_ref[seeing, columns])
                value_part += dot(high_ref[head, spot(number), seeing], g_ref[seeing, columns])
            grad_ref[spot(number), :HD] = key_part * SCALE
            grad_ref[spot(number), HD:] = value_part

    square = pltpu.VMEM((heads, rows, rows), jnp.bfloat16)
    return pl.pallas_call(
        body,
        out_shape=(
            jax.ShapeDtypeStruct((rows, width + 2 * HD), jnp.bfloat16),
            jax.ShapeDtypeStruct((rows, 2 * HD), jnp.float32),
        ),
        in_specs=[VMEM] * (7 + levels),
        out_specs=(VMEM,) * 2,
        scratch_shapes=[pltpu.VMEM((HD, rows + levels * BLK), jnp.bfloat16), square, square],
        compiler_params=params(14),
        cost_estimate=cost(3 * total + heads * row_tiles * levels, 2 << 20),
        name="own_part",
    )(queries, grad_out, own, weights, grad_probs, low, coef, *blocks)


def add_returned(block_index, joined, gradients, returned, ctx_count):
    levels, width = len(returned), joined.shape[1] - gradients.shape[1]

    def body(index_ref, joined_ref, grad_ref, *refs):
        out_ref, total_ref = refs[levels:]
        ctx_index = lax.axis_index("ctx")
        for level_num in range(levels):
            start = block_start(index_ref, ctx_index, level_num, ctx_count)
            total_ref[pl.ds(start, BLK), :] += refs[level_num][...].astype(jnp.float32)
        out_ref[:, width:] = total_ref[...].astype(jnp.bfloat16)

    return pl.pallas_call(
        body,
        out_shape=tuple(jax.ShapeDtypeStruct(each.shape, each.dtype) for each in (joined, gradients)),
        in_specs=[SMEM] + [VMEM] * (levels + 2),
        out_specs=(VMEM, VMEM),
        input_output_aliases={1: 0, 2: 1},
        compiler_params=params(6),
        name="add_returned",
    )(block_index, joined, gradients, *returned)[0]


def lay_out(gathered, width):
    count, token_rows, _ = gathered.shape

    def body(in_ref, query_ref, key_ref, value_ref):
        for number in range(count):
            query_ref[:, number * width : (number + 1) * width] = in_ref[number, :, :width]
        for number in range(count // 2):
            total = in_ref[2 * number, :, width:].astype(jnp.float32)
            total += in_ref[2 * number + 1, :, width:].astype(jnp.float32)
            total = total.astype(jnp.bfloat16)
            key_ref[:, number * HD : (number + 1) * HD] = total[:, :HD]
            value_ref[:, number * HD : (number + 1) * HD] = total[:, HD:]

    shape = jax.ShapeDtypeStruct((token_rows, count // 2 * HD), gathered.dtype)
    return pl.pallas_call(
        body,
        out_shape=(jax.ShapeDtypeStruct((token_rows, count * width), gathered.dtype), shape, shape),
        in_specs=[VMEM],
        out_specs=(VMEM,) * 3,
        compiler_params=params(6),
        name="lay_out",
    )(gathered)


def on_device(queries, keys, values, grad_out, block_index):
    ctx_count = lax.axis_size("ctx")
    head_count = lax.axis_size("head")
    levels = ctx_count.bit_length() - 1
    rows, width = queries.shape
    block_index = block_index.T
    hbm = [pltpu.with_memory_space_constraint(each, pltpu.HBM) for each in (block_index, keys, values)]
    own, *sends = gather_blocks(*hbm, ctx_count, levels)
    blocks = [rotate(sends[level_num], "ctx", 2**level_num) for level_num in range(levels)]
    queries_t, grad_t, weights, grad_probs, stats = own_scores(queries, grad_out, own)
    scored = [block_scores(queries_t, grad_t, block) for block in blocks]
    *parts, low, coef = partner_part(queries, grad_out, stats, scored)
    returned = [rotate(parts[level_num], "ctx", -(2**level_num)) for level_num in range(levels)]
    joined, gradients = own_part(queries, grad_out, own, blocks, weights, grad_probs, low, coef)
    joined = add_returned(block_index, joined, gradients, returned, ctx_count)
    split = joined.reshape(head_count, rows // head_count, joined.shape[1])
    gathered = lax.all_to_all(split, "head", split_axis=0, concat_axis=0, tiled=True)
    return tuple(lay_out(gathered, width))


def solution(mesh):
    placed = (P("ctx", "head"), P("ctx", None), P("ctx", None), P("ctx", "head"), P())
    return jax.shard_map(
        on_device,
        mesh=mesh,
        in_specs=placed,
        out_specs=(P(("ctx", "head"), None), P(("ctx", "head"), None), P(("ctx", "head"), None)),
        check_vma=False,
    )
```

```python
import jax
import jax.numpy as jnp
from jax import lax
from jax.experimental import pallas as pl
from jax.experimental.pallas import tpu as pltpu
from jax.sharding import PartitionSpec as P

HD = 128
BLK = 256
NEG = -1e30
SCALE = HD**-0.5
FACTOR = SCALE * 1.4426950408889634
HBM = pl.BlockSpec(memory_space=pltpu.HBM)
VMEM = pl.BlockSpec(memory_space=pltpu.VMEM)
SMEM = pl.BlockSpec(memory_space=pltpu.SMEM)


def rotate(value, axis, steps):
    count = lax.axis_size(axis)
    return lax.ppermute(value, axis, [(source, (source + steps) % count) for source in range(count)])


def swap(value, axis):
    return lax.ppermute(value, axis, [(source, source ^ 1) for source in range(lax.axis_size(axis))])


def block_start(index_ref, ctx_index, level_num, ctx_count):
    target = jnp.minimum(ctx_index + 2**level_num, ctx_count - 1)
    return pl.multiple_of(index_ref[level_num, target] * BLK, BLK)


def gather_blocks(block_index, keys, values, ctx_count, levels):
    def body(index_hbm, key_ref, value_ref, own_ref, *refs):
        sends, index_ref, sems = refs[:levels], refs[levels], refs[levels + 1]
        begin = pl.multiple_of(lax.axis_index("head") // 2 * HD, HD)
        started = [pltpu.make_async_copy(index_hbm, index_ref, sems.at[2])]
        for half, source in ((0, key_ref), (1, value_ref)):
            started.append(
                pltpu.make_async_copy(
                    source.at[:, pl.ds(begin, HD)], own_ref.at[:, half * HD : (half + 1) * HD], sems.at[half]
                )
            )
        for copy in started:
            copy.start()
        for copy in started:
            copy.wait()
        ctx_index = lax.axis_index("ctx")
        for level_num in range(levels):
            start = block_start(index_ref, ctx_index, level_num, ctx_count)
            sends[level_num][...] = own_ref[pl.ds(start, BLK), :]

    return pl.pallas_call(
        body,
        out_shape=(jax.ShapeDtypeStruct((keys.shape[0], 2 * HD), keys.dtype),)
        + (jax.ShapeDtypeStruct((BLK, 2 * HD), keys.dtype),) * levels,
        in_specs=[HBM, HBM, HBM],
        out_specs=(VMEM,) * (levels + 1),
        scratch_shapes=[pltpu.SMEM(block_index.shape, jnp.int32), pltpu.SemaphoreType.DMA((3,))],
        compiler_params=params(4),
        name="gather_blocks",
    )(block_index, keys, values)


def dot(left, right):
    return jnp.dot(left, right, preferred_element_type=jnp.float32)


def spot(number):
    return slice(number * BLK, (number + 1) * BLK)


def params(mib):
    return pltpu.CompilerParams(vmem_limit_bytes=mib << 20)


def cost(dots, nbytes):
    return pl.CostEstimate(flops=dots * 2 * BLK * BLK * HD, bytes_accessed=nbytes, transcendentals=0)


def pairs(row_tiles):
    return [(part, number) for part in range(row_tiles) for number in range(part + 1)]


def score_tile(key_tile, value_tile, query_t, grad_t, seen=None):
    scores = dot(key_tile, query_t)
    if seen is not None:
        scores = jnp.where(seen, scores, NEG)
    top = jnp.max(scores, axis=0, keepdims=True) * FACTOR
    weights = jnp.exp2(scores * FACTOR - top)
    grad_probs = dot(value_tile, grad_t)
    total = jnp.sum(weights, axis=0, keepdims=True)
    product = jnp.sum(weights * grad_probs, axis=0, keepdims=True)
    return weights, grad_probs, (top, total, product)


def own_scores(queries, grad_out, own):
    rows, width = queries.shape
    row_tiles, heads = rows // BLK, width // HD
    places = pairs(row_tiles)
    total = heads * len(places)

    def body(q_ref, g_ref, own_ref, both_ref, qt_ref, gt_ref, weight_ref, prob_ref, stat_ref):
        both_ref[0], both_ref[1] = q_ref[...], g_ref[...]
        key_at = lax.broadcasted_iota(jnp.int32, (BLK, BLK), 0)
        causal = key_at <= lax.broadcasted_iota(jnp.int32, (BLK, BLK), 1)
        for head in range(heads):
            columns = slice(head * HD, (head + 1) * HD)
            for part in range(row_tiles):
                query_t, grad_t = q_ref[spot(part), columns].T, g_ref[spot(part), columns].T
                qt_ref[columns, spot(part)] = query_t
                gt_ref[columns, spot(part)] = grad_t
                for number in range(part + 1):
                    place = head * len(places) + places.index((part, number))
                    weight_ref[place], prob_ref[place], found = score_tile(
                        own_ref[spot(number), :HD],
                        own_ref[spot(number), HD:],
                        query_t,
                        grad_t,
                        causal if number == part else None,
                    )
                    for row, each in enumerate(found):
                        stat_ref[row, place : place + 1] = each

    tiles = jax.ShapeDtypeStruct((total, BLK, BLK), jnp.float32)
    turned = jax.ShapeDtypeStruct((width, rows), jnp.bfloat16)
    return pl.pallas_call(
        body,
        out_shape=(
            jax.ShapeDtypeStruct((2, rows, width), jnp.bfloat16),
            turned,
            turned,
            tiles,
            tiles,
            jax.ShapeDtypeStruct((3, total, BLK), jnp.float32),
        ),
        in_specs=[VMEM] * 3,
        out_specs=(VMEM,) * 6,
        compiler_params=params(8),
        cost_estimate=cost(2 * total, 2 << 20),
        name="own_scores",
    )(queries, grad_out, own)


def block_scores(queries_t, grad_t, block):
    width, rows = queries_t.shape
    row_tiles, heads = rows // BLK, width // HD

    def body(qt_ref, gt_ref, block_ref, weight_ref, prob_ref, stat_ref):
        for head in range(heads):
            columns = slice(head * HD, (head + 1) * HD)
            for part in range(row_tiles):
                place = head * row_tiles + part
                weight_ref[place], prob_ref[place], found = score_tile(
                    block_ref[:, :HD], block_ref[:, HD:], qt_ref[columns, spot(part)], gt_ref[columns, spot(part)]
                )
                for row, each in enumerate(found):
                    stat_ref[row, place : place + 1] = each

    tiles = jax.ShapeDtypeStruct((heads * row_tiles, BLK, BLK), jnp.float32)
    return pl.pallas_call(
        body,
        out_shape=(tiles, tiles, jax.ShapeDtypeStruct((3, heads * row_tiles, BLK), jnp.float32)),
        in_specs=[VMEM] * 3,
        out_specs=(VMEM,) * 3,
        compiler_params=params(8),
        cost_estimate=cost(2 * heads * row_tiles, 2 << 20),
        name="block_scores",
    )(queries_t, grad_t, block)


def kinds():
    keep = lax.axis_index("head") % 2
    scales = [jnp.where(kind == 0, SCALE, 1.0) for kind in (keep, 1 - keep)]
    return keep, 1 - keep, scales[0], scales[1]


def partner_part(both, own_stats, scored):
    _, rows, width = both.shape
    levels, row_tiles, heads = len(scored), rows // BLK, width // HD
    places = pairs(row_tiles)
    total = heads * len(places)

    def body(both_ref, own_ref, *refs):
        scored_refs = [refs[3 * level_num : 3 * level_num + 3] for level_num in range(levels)]
        send_ref, held_ref, coef_ref = refs[3 * levels :]
        ctx_index = lax.axis_index("ctx")
        live = [ctx_index >= 2**level_num for level_num in range(levels)]
        ratio_of = {}
        for head in range(heads):
            for part in range(row_tiles):
                at = head * row_tiles + part
                tops, sums, products = [], [], []
                for level_num in range(levels):
                    stat_ref = scored_refs[level_num][2]
                    tops.append(jnp.where(live[level_num], stat_ref[0, at : at + 1], NEG))
                    sums.append(stat_ref[1, at : at + 1])
                    products.append(stat_ref[2, at : at + 1])
                first = head * len(places) + places.index((part, 0))
                for place in range(first, first + part + 1):
                    tops.append(own_ref[0, place : place + 1])
                    sums.append(own_ref[1, place : place + 1])
                    products.append(own_ref[2, place : place + 1])
                row_max = tops[0]
                for top in tops[1:]:
                    row_max = jnp.maximum(row_max, top)
                ratios = [jnp.exp2(top - row_max) for top in tops]
                inverse = 1.0 / sum(each * ratio for each, ratio in zip(sums, ratios))
                delta = sum(each * ratio for each, ratio in zip(products, ratios)) * inverse
                for number in range(part + 1):
                    coef_ref[first + number : first + number + 1] = ratios[levels + number] * inverse
                coef_ref[total + at : total + at + 1] = delta
                ratio_of[at] = [ratio * inverse for ratio in ratios[:levels]], delta
        _, send, _, scale = kinds()
        for level_num in range(levels):
            weight_ref, prob_ref, _ = scored_refs[level_num]
            sent = 0.0
            for head in range(heads):
                for part in range(row_tiles):
                    at = head * row_tiles + part
                    ratios, delta = ratio_of[at]
                    probs = weight_ref[at] * ratios[level_num]
                    low = (probs * (prob_ref[at] - delta)).astype(jnp.bfloat16)
                    held_ref[0, head, spot(level_num), spot(part)] = low
                    held_ref[1, head, spot(level_num), spot(part)] = probs.astype(jnp.bfloat16)
                columns = slice(head * HD, (head + 1) * HD)
                sent += dot(held_ref[send, head, spot(level_num)], both_ref[send, :, columns])
            send_ref[spot(level_num)] = (sent * scale).astype(jnp.bfloat16)

    return pl.pallas_call(
        body,
        out_shape=(
            jax.ShapeDtypeStruct((levels * BLK, HD), jnp.bfloat16),
            jax.ShapeDtypeStruct((2, heads, levels * BLK, rows), jnp.bfloat16),
            jax.ShapeDtypeStruct((total + heads * row_tiles, BLK), jnp.float32),
        ),
        in_specs=[VMEM] * (2 + 3 * levels),
        out_specs=(VMEM,) * 3,
        compiler_params=params(6),
        cost_estimate=cost(2 * heads * row_tiles * levels, 2 << 20),
        name="partner_part",
    )(both, own_stats, *[each for level in scored for each in level])


def own_part(both, own, blocks, weights, grad_probs, held, coef):
    _, rows, width = both.shape
    levels, row_tiles, heads = len(blocks), rows // BLK, width // HD
    places = pairs(row_tiles)
    total = heads * len(places)

    def body(both_ref, own_ref, weight_ref, prob_ref, held_ref, coef_ref, *refs):
        block_refs = refs[:levels]
        part_ref, keep_ref, send_ref, joined_ref, kt_ref, own_held_ref = refs[levels:]
        keep, send, keep_scale, send_scale = kinds()
        for level_num in range(levels):
            kept = 0.0
            for head in range(heads):
                columns = slice(head * HD, (head + 1) * HD)
                kept += dot(held_ref[keep, head, spot(level_num)], both_ref[keep, :, columns])
            part_ref[spot(level_num)] = kept * keep_scale
        for number in range(row_tiles):
            kt_ref[:, spot(number)] = own_ref[spot(number), :HD].T
        for level_num in range(levels):
            kt_ref[:, spot(row_tiles + level_num)] = block_refs[level_num][:, :HD].T
        for head in range(heads):
            columns = slice(head * HD, (head + 1) * HD)
            for part in range(row_tiles):
                at = total + head * row_tiles + part
                delta = coef_ref[at : at + 1]
                for number in range(part + 1):
                    place = head * len(places) + places.index((part, number))
                    probs = weight_ref[place] * coef_ref[place : place + 1]
                    low = (probs * (prob_ref[place] - delta)).astype(jnp.bfloat16)
                    own_held_ref[0, head, spot(number), spot(part)] = low
                    own_held_ref[1, head, spot(number), spot(part)] = probs.astype(jnp.bfloat16)
                dq_t = dot(kt_ref[:, rows:], held_ref[0, head, :, spot(part)])
                seen = slice(0, (part + 1) * BLK)
                dq_t += dot(kt_ref[:, seen], own_held_ref[0, head, seen, spot(part)])
                joined_ref[spot(part), columns] = (dq_t * SCALE).T.astype(jnp.bfloat16)
        for number in range(row_tiles):
            kept = sent = 0.0
            seeing = slice(number * BLK, rows)
            for head in range(heads):
                columns = slice(head * HD, (head + 1) * HD)
                kept += dot(own_held_ref[keep, head, spot(number), seeing], both_ref[keep, seeing, columns])
                sent += dot(own_held_ref[send, head, spot(number), seeing], both_ref[send, seeing, columns])
            keep_ref[spot(number)] = kept * keep_scale
            send_ref[spot(number)] = (sent * send_scale).astype(jnp.bfloat16)

    return pl.pallas_call(
        body,
        out_shape=(
            jax.ShapeDtypeStruct((levels * BLK, HD), jnp.float32),
            jax.ShapeDtypeStruct((rows, HD), jnp.float32),
            jax.ShapeDtypeStruct((rows, HD), jnp.bfloat16),
            jax.ShapeDtypeStruct((rows, width + HD), jnp.bfloat16),
        ),
        in_specs=[VMEM] * (6 + levels),
        out_specs=(VMEM,) * 4,
        scratch_shapes=[
            pltpu.VMEM((HD, rows + levels * BLK), jnp.bfloat16),
            pltpu.VMEM((2, heads, rows, rows), jnp.bfloat16),
        ],
        compiler_params=params(14),
        cost_estimate=cost(3 * total + 2 * heads * row_tiles * levels, 2 << 20),
        name="own_part",
    )(both, own, weights, grad_probs, held, coef, *blocks)


def pair_parts(kept, received, levels):
    def body(kept_ref, received_ref, *part_refs):
        for level_num in range(levels):
            total = kept_ref[spot(level_num)] + received_ref[spot(level_num)].astype(jnp.float32)
            part_refs[level_num][...] = total.astype(jnp.bfloat16)

    return pl.pallas_call(
        body,
        out_shape=(jax.ShapeDtypeStruct((BLK, HD), jnp.bfloat16),) * levels,
        in_specs=[VMEM] * 2,
        out_specs=(VMEM,) * levels,
        compiler_params=params(6),
        name="pair_parts",
    )(kept, received)


def add_returned(block_index, joined, kept, received, returned, ctx_count):
    levels, width = len(returned), joined.shape[1] - HD

    def body(index_ref, joined_ref, kept_ref, received_ref, *refs):
        out_ref, total_ref = refs[levels:]
        ctx_index = lax.axis_index("ctx")
        total_ref[...] = kept_ref[...] + received_ref[...].astype(jnp.float32)
        for level_num in range(levels):
            start = block_start(index_ref, ctx_index, level_num, ctx_count)
            total_ref[pl.ds(start, BLK), :] += refs[level_num][...].astype(jnp.float32)
        out_ref[:, width:] = total_ref[...].astype(jnp.bfloat16)

    return pl.pallas_call(
        body,
        out_shape=jax.ShapeDtypeStruct(joined.shape, joined.dtype),
        in_specs=[SMEM] + [VMEM] * (levels + 3),
        out_specs=VMEM,
        scratch_shapes=[pltpu.VMEM(kept.shape, jnp.float32)],
        input_output_aliases={1: 0},
        compiler_params=params(6),
        name="add_returned",
    )(block_index, joined, kept, received, *returned)


def lay_out(gathered, width):
    count, token_rows, _ = gathered.shape

    def body(in_ref, query_ref, key_ref, value_ref):
        for number in range(count):
            query_ref[:, number * width : (number + 1) * width] = in_ref[number, :, :width]
            kind_ref = key_ref if number % 2 == 0 else value_ref
            group = number // 2
            kind_ref[:, group * HD : (group + 1) * HD] = in_ref[number, :, width:]

    shape = jax.ShapeDtypeStruct((token_rows, count // 2 * HD), gathered.dtype)
    return pl.pallas_call(
        body,
        out_shape=(jax.ShapeDtypeStruct((token_rows, count * width), gathered.dtype), shape, shape),
        in_specs=[VMEM],
        out_specs=(VMEM,) * 3,
        compiler_params=params(6),
        name="lay_out",
    )(gathered)


def on_device(queries, keys, values, grad_out, block_index):
    ctx_count = lax.axis_size("ctx")
    head_count = lax.axis_size("head")
    levels = ctx_count.bit_length() - 1
    rows, width = queries.shape
    block_index = block_index.T
    hbm = [pltpu.with_memory_space_constraint(each, pltpu.HBM) for each in (block_index, keys, values)]
    own, *sends = gather_blocks(*hbm, ctx_count, levels)
    blocks = [rotate(sends[level_num], "ctx", 2**level_num) for level_num in range(levels)]
    both, queries_t, grad_t, weights, grad_probs, stats = own_scores(queries, grad_out, own)
    scored = [block_scores(queries_t, grad_t, block) for block in blocks]
    sent, held, coef = partner_part(both, stats, scored)
    received = swap(sent, "head")
    part_kept, own_kept, own_sent, joined = own_part(both, own, blocks, weights, grad_probs, held, coef)
    own_received = swap(own_sent, "head")
    parts = pair_parts(part_kept, received, levels)
    returned = [rotate(parts[level_num], "ctx", -(2**level_num)) for level_num in range(levels)]
    joined = add_returned(block_index, joined, own_kept, own_received, returned, ctx_count)
    split = joined.reshape(head_count, rows // head_count, joined.shape[1])
    gathered = lax.all_to_all(split, "head", split_axis=0, concat_axis=0, tiled=True)
    return tuple(lay_out(gathered, width))


def solution(mesh):
    placed = (P("ctx", "head"), P("ctx", None), P("ctx", None), P("ctx", "head"), P())
    return jax.shard_map(
        on_device,
        mesh=mesh,
        in_specs=placed,
        out_specs=(P(("ctx", "head"), None), P(("ctx", "head"), None), P(("ctx", "head"), None)),
        check_vma=False,
    )
```

```python
import jax
import jax.numpy as jnp
from jax import lax
from jax.experimental import pallas as pl
from jax.experimental.pallas import tpu as pltpu
from jax.sharding import PartitionSpec as P


HD = 128
BLK = 256
NEG = -1e30
SCALE = HD**-0.5
FACTOR = SCALE * 1.4426950408889634
HBM = pl.BlockSpec(memory_space=pltpu.HBM)
VMEM = pl.BlockSpec(memory_space=pltpu.VMEM)
SMEM = pl.BlockSpec(memory_space=pltpu.SMEM)


def rotate(value, axis, steps):
    count = lax.axis_size(axis)
    return lax.ppermute(value, axis, [(source, (source + steps) % count) for source in range(count)])


def swap(value, axis):
    return lax.ppermute(value, axis, [(source, source ^ 1) for source in range(lax.axis_size(axis))])


def block_start(index_ref, ctx_index, level_num, ctx_count):
    target = jnp.minimum(ctx_index + 2**level_num, ctx_count - 1)
    return pl.multiple_of(index_ref[level_num, target] * BLK, BLK)


def gather_blocks(block_index, keys, values, ctx_count, levels):
    def body(index_hbm, key_ref, value_ref, own_ref, *refs):
        sends, index_ref, sems = refs[:levels], refs[levels], refs[levels + 1]
        begin = pl.multiple_of(lax.axis_index("head") // 2 * HD, HD)
        started = [pltpu.make_async_copy(index_hbm, index_ref, sems.at[2])]
        for half, source in ((0, key_ref), (1, value_ref)):
            started.append(
                pltpu.make_async_copy(
                    source.at[:, pl.ds(begin, HD)], own_ref.at[:, half * HD : (half + 1) * HD], sems.at[half]
                )
            )
        for copy in started:
            copy.start()
        for copy in started:
            copy.wait()
        ctx_index = lax.axis_index("ctx")
        for level_num in range(levels):
            start = block_start(index_ref, ctx_index, level_num, ctx_count)
            sends[level_num][...] = own_ref[pl.ds(start, BLK), :]

    return pl.pallas_call(
        body,
        out_shape=(jax.ShapeDtypeStruct((keys.shape[0], 2 * HD), keys.dtype),)
        + (jax.ShapeDtypeStruct((BLK, 2 * HD), keys.dtype),) * levels,
        in_specs=[HBM, HBM, HBM],
        out_specs=(VMEM,) * (levels + 1),
        scratch_shapes=[pltpu.SMEM(block_index.shape, jnp.int32), pltpu.SemaphoreType.DMA((3,))],
        compiler_params=params(4),
        name="gather_blocks",
    )(block_index, keys, values)


def dot(left, right):
    return jnp.dot(left, right, preferred_element_type=jnp.float32)


def spot(number):
    return slice(number * BLK, (number + 1) * BLK)


def params(mib):
    return pltpu.CompilerParams(vmem_limit_bytes=mib << 20)


def cost(dots, nbytes):
    return pl.CostEstimate(flops=dots * 2 * BLK * BLK * HD, bytes_accessed=nbytes, transcendentals=0)


def pairs(row_tiles):
    return [(part, number) for part in range(row_tiles) for number in range(part + 1)]


def score_tile(key_tile, value_tile, query_t, grad_t, seen=None):
    scores = dot(key_tile, query_t)
    if seen is not None:
        scores = jnp.where(seen, scores, NEG)
    top = jnp.max(scores, axis=0, keepdims=True) * FACTOR
    weights = jnp.exp2(scores * FACTOR - top)
    grad_probs = dot(value_tile, grad_t)
    total = jnp.sum(weights, axis=0, keepdims=True)
    product = jnp.sum(weights * grad_probs, axis=0, keepdims=True)
    return weights, grad_probs, (top, total, product)


def own_scores(queries, grad_out, own):
    rows, width = queries.shape
    row_tiles, heads = rows // BLK, width // HD
    places = pairs(row_tiles)
    total = heads * len(places)

    def body(q_ref, g_ref, own_ref, both_ref, qt_ref, gt_ref, weight_ref, prob_ref, stat_ref):
        both_ref[0], both_ref[1] = q_ref[...], g_ref[...]
        key_at = lax.broadcasted_iota(jnp.int32, (BLK, BLK), 0)
        causal = key_at <= lax.broadcasted_iota(jnp.int32, (BLK, BLK), 1)
        for head in range(heads):
            columns = slice(head * HD, (head + 1) * HD)
            for part in range(row_tiles):
                query_t, grad_t = q_ref[spot(part), columns].T, g_ref[spot(part), columns].T
                qt_ref[columns, spot(part)] = query_t
                gt_ref[columns, spot(part)] = grad_t
                for number in range(part + 1):
                    place = head * len(places) + places.index((part, number))
                    weight_ref[place], prob_ref[place], found = score_tile(
                        own_ref[spot(number), :HD],
                        own_ref[spot(number), HD:],
                        query_t,
                        grad_t,
                        causal if number == part else None,
                    )
                    for row, each in enumerate(found):
                        stat_ref[row, place : place + 1] = each

    tiles = jax.ShapeDtypeStruct((total, BLK, BLK), jnp.float32)
    turned = jax.ShapeDtypeStruct((width, rows), jnp.bfloat16)
    return pl.pallas_call(
        body,
        out_shape=(
            jax.ShapeDtypeStruct((2, rows, width), jnp.bfloat16),
            turned,
            turned,
            tiles,
            tiles,
            jax.ShapeDtypeStruct((3, total, BLK), jnp.float32),
        ),
        in_specs=[VMEM] * 3,
        out_specs=(VMEM,) * 6,
        compiler_params=params(8),
        cost_estimate=cost(2 * total, 2 << 20),
        name="own_scores",
    )(queries, grad_out, own)


def block_scores(queries_t, grad_t, block):
    width, rows = queries_t.shape
    row_tiles, heads = rows // BLK, width // HD

    def body(qt_ref, gt_ref, block_ref, weight_ref, prob_ref, stat_ref):
        for head in range(heads):
            columns = slice(head * HD, (head + 1) * HD)
            for part in range(row_tiles):
                place = head * row_tiles + part
                weight_ref[place], prob_ref[place], found = score_tile(
                    block_ref[:, :HD], block_ref[:, HD:], qt_ref[columns, spot(part)], gt_ref[columns, spot(part)]
                )
                for row, each in enumerate(found):
                    stat_ref[row, place : place + 1] = each

    tiles = jax.ShapeDtypeStruct((heads * row_tiles, BLK, BLK), jnp.float32)
    return pl.pallas_call(
        body,
        out_shape=(tiles, tiles, jax.ShapeDtypeStruct((3, heads * row_tiles, BLK), jnp.float32)),
        in_specs=[VMEM] * 3,
        out_specs=(VMEM,) * 3,
        compiler_params=params(8),
        cost_estimate=cost(2 * heads * row_tiles, 2 << 20),
        name="block_scores",
    )(queries_t, grad_t, block)


def kinds():
    keep = lax.axis_index("head") % 2
    scales = [jnp.where(kind == 0, SCALE, 1.0) for kind in (keep, 1 - keep)]
    return keep, 1 - keep, scales[0], scales[1]


def partner_part(both, own_stats, scored):
    _, rows, width = both.shape
    levels, row_tiles, heads = len(scored), rows // BLK, width // HD
    places = pairs(row_tiles)
    total = heads * len(places)

    def body(both_ref, own_ref, *refs):
        scored_refs = [refs[3 * level_num : 3 * level_num + 3] for level_num in range(levels)]
        send_ref, held_ref, coef_ref, chosen_ref = refs[3 * levels :]
        ctx_index = lax.axis_index("ctx")
        live = [ctx_index >= 2**level_num for level_num in range(levels)]
        ratio_of = {}
        for head in range(heads):
            for part in range(row_tiles):
                at = head * row_tiles + part
                tops, sums, products = [], [], []
                for level_num in range(levels):
                    stat_ref = scored_refs[level_num][2]
                    tops.append(jnp.where(live[level_num], stat_ref[0, at : at + 1], NEG))
                    sums.append(stat_ref[1, at : at + 1])
                    products.append(stat_ref[2, at : at + 1])
                first = head * len(places) + places.index((part, 0))
                for place in range(first, first + part + 1):
                    tops.append(own_ref[0, place : place + 1])
                    sums.append(own_ref[1, place : place + 1])
                    products.append(own_ref[2, place : place + 1])
                row_max = tops[0]
                for top in tops[1:]:
                    row_max = jnp.maximum(row_max, top)
                ratios = [jnp.exp2(top - row_max) for top in tops]
                inverse = 1.0 / sum(each * ratio for each, ratio in zip(sums, ratios))
                delta = sum(each * ratio for each, ratio in zip(products, ratios)) * inverse
                for number in range(part + 1):
                    coef_ref[first + number : first + number + 1] = ratios[levels + number] * inverse
                coef_ref[total + at : total + at + 1] = delta
                ratio_of[at] = [ratio * inverse for ratio in ratios[:levels]], delta
        _, send, _, scale = kinds()
        for level_num in range(levels):
            weight_ref, prob_ref, _ = scored_refs[level_num]
            sent = 0.0
            for head in range(heads):
                for part in range(row_tiles):
                    at = head * row_tiles + part
                    ratios, delta = ratio_of[at]
                    probs = weight_ref[at] * ratios[level_num]
                    low = (probs * (prob_ref[at] - delta)).astype(jnp.bfloat16)
                    probs = probs.astype(jnp.bfloat16)
                    held_ref[0, head, spot(level_num), spot(part)] = low
                    held_ref[1, head, spot(level_num), spot(part)] = probs
                    chosen_ref[head, spot(level_num), spot(part)] = jnp.where(send == 0, low, probs)
                columns = slice(head * HD, (head + 1) * HD)
                sent += dot(chosen_ref[head, spot(level_num)], both_ref[send, :, columns])
            send_ref[spot(level_num)] = (sent * scale).astype(jnp.bfloat16)

    return pl.pallas_call(
        body,
        out_shape=(
            jax.ShapeDtypeStruct((levels * BLK, HD), jnp.bfloat16),
            jax.ShapeDtypeStruct((2, heads, levels * BLK, rows), jnp.bfloat16),
            jax.ShapeDtypeStruct((total + heads * row_tiles, BLK), jnp.float32),
        ),
        in_specs=[VMEM] * (2 + 3 * levels),
        out_specs=(VMEM,) * 3,
        scratch_shapes=[pltpu.VMEM((heads, levels * BLK, rows), jnp.bfloat16)],
        compiler_params=params(8),
        cost_estimate=cost(2 * heads * row_tiles * levels, 2 << 20),
        name="partner_part",
    )(both, own_stats, *[each for level in scored for each in level])


def own_part(both, own, blocks, weights, grad_probs, held, coef):
    _, rows, width = both.shape
    levels, row_tiles, heads = len(blocks), rows // BLK, width // HD
    places = pairs(row_tiles)
    total = heads * len(places)

    def body(both_ref, own_ref, weight_ref, prob_ref, held_ref, coef_ref, *refs):
        block_refs = refs[:levels]
        part_ref, keep_ref, send_ref, dq_ref, kt_ref, own_held_ref = refs[levels:]
        keep, send, keep_scale, send_scale = kinds()
        for level_num in range(levels):
            kept = 0.0
            for head in range(heads):
                columns = slice(head * HD, (head + 1) * HD)
                kept += dot(held_ref[keep, head, spot(level_num)], both_ref[keep, :, columns])
            part_ref[spot(level_num)] = kept * keep_scale
        for number in range(row_tiles):
            kt_ref[:, spot(number)] = own_ref[spot(number), :HD].T
        for level_num in range(levels):
            kt_ref[:, spot(row_tiles + level_num)] = block_refs[level_num][:, :HD].T
        for head in range(heads):
            columns = slice(head * HD, (head + 1) * HD)
            for part in range(row_tiles):
                at = total + head * row_tiles + part
                delta = coef_ref[at : at + 1]
                for number in range(part + 1):
                    place = head * len(places) + places.index((part, number))
                    probs = weight_ref[place] * coef_ref[place : place + 1]
                    low = (probs * (prob_ref[place] - delta)).astype(jnp.bfloat16)
                    own_held_ref[0, head, spot(number), spot(part)] = low
                    own_held_ref[1, head, spot(number), spot(part)] = probs.astype(jnp.bfloat16)
                dq_t = dot(kt_ref[:, rows:], held_ref[0, head, :, spot(part)])
                seen = slice(0, (part + 1) * BLK)
                dq_t += dot(kt_ref[:, seen], own_held_ref[0, head, seen, spot(part)])
                dq_ref[spot(part), columns] = (dq_t * SCALE).T.astype(jnp.bfloat16)
        for number in range(row_tiles):
            kept = sent = 0.0
            seeing = slice(number * BLK, rows)
            for head in range(heads):
                columns = slice(head * HD, (head + 1) * HD)
                kept += dot(own_held_ref[keep, head, spot(number), seeing], both_ref[keep, seeing, columns])
                sent += dot(own_held_ref[send, head, spot(number), seeing], both_ref[send, seeing, columns])
            keep_ref[spot(number)] = kept * keep_scale
            send_ref[spot(number)] = (sent * send_scale).astype(jnp.bfloat16)

    return pl.pallas_call(
        body,
        out_shape=(
            jax.ShapeDtypeStruct((levels * BLK, HD), jnp.float32),
            jax.ShapeDtypeStruct((rows, HD), jnp.float32),
            jax.ShapeDtypeStruct((rows, HD), jnp.bfloat16),
            jax.ShapeDtypeStruct((rows, width), jnp.bfloat16),
        ),
        in_specs=[VMEM] * (6 + levels),
        out_specs=(VMEM,) * 4,
        scratch_shapes=[
            pltpu.VMEM((HD, rows + levels * BLK), jnp.bfloat16),
            pltpu.VMEM((2, heads, rows, rows), jnp.bfloat16),
        ],
        compiler_params=params(14),
        cost_estimate=cost(3 * total + 2 * heads * row_tiles * levels, 2 << 20),
        name="own_part",
    )(both, own, weights, grad_probs, held, coef, *blocks)


def pair_parts(kept, received, levels):
    def body(kept_ref, received_ref, *part_refs):
        for level_num in range(levels):
            total = kept_ref[spot(level_num)] + received_ref[spot(level_num)].astype(jnp.float32)
            part_refs[level_num][...] = total.astype(jnp.bfloat16)

    return pl.pallas_call(
        body,
        out_shape=(jax.ShapeDtypeStruct((BLK, HD), jnp.bfloat16),) * levels,
        in_specs=[VMEM] * 2,
        out_specs=(VMEM,) * levels,
        compiler_params=params(6),
        name="pair_parts",
    )(kept, received)


def add_returned(block_index, kept, received, returned, ctx_count):
    levels = len(returned)

    def body(index_ref, kept_ref, received_ref, *refs):
        out_ref, total_ref = refs[levels:]
        ctx_index = lax.axis_index("ctx")
        total_ref[...] = kept_ref[...] + received_ref[...].astype(jnp.float32)
        for level_num in range(levels):
            start = block_start(index_ref, ctx_index, level_num, ctx_count)
            total_ref[pl.ds(start, BLK), :] += refs[level_num][...].astype(jnp.float32)
        out_ref[...] = total_ref[...].astype(jnp.bfloat16)

    return pl.pallas_call(
        body,
        out_shape=jax.ShapeDtypeStruct(kept.shape, jnp.bfloat16),
        in_specs=[SMEM] + [VMEM] * (levels + 2),
        out_specs=VMEM,
        scratch_shapes=[pltpu.VMEM(kept.shape, jnp.float32)],
        compiler_params=params(6),
        name="add_returned",
    )(block_index, kept, received, *returned)


def lay_queries(gathered):
    count, token_rows, width = gathered.shape

    def body(in_ref, out_ref):
        for number in range(count):
            out_ref[:, number * width : (number + 1) * width] = in_ref[number]

    return pl.pallas_call(
        body,
        out_shape=jax.ShapeDtypeStruct((token_rows, count * width), gathered.dtype),
        in_specs=[VMEM],
        out_specs=VMEM,
        compiler_params=params(6),
        name="lay_queries",
    )(gathered)


def lay_keys(gathered):
    count, token_rows, _ = gathered.shape

    def body(in_ref, key_ref, value_ref):
        for number in range(count):
            kind_ref = key_ref if number % 2 == 0 else value_ref
            group = number // 2
            kind_ref[:, group * HD : (group + 1) * HD] = in_ref[number]

    shape = jax.ShapeDtypeStruct((token_rows, count // 2 * HD), gathered.dtype)
    return pl.pallas_call(
        body,
        out_shape=(shape, shape),
        in_specs=[VMEM],
        out_specs=(VMEM,) * 2,
        compiler_params=params(6),
        name="lay_keys",
    )(gathered)


def spread(value, head_count):
    split = value.reshape(head_count, value.shape[0] // head_count, value.shape[1])
    return lax.all_to_all(split, "head", split_axis=0, concat_axis=0, tiled=True)


def on_device(queries, keys, values, grad_out, block_index):
    ctx_count = lax.axis_size("ctx")
    head_count = lax.axis_size("head")
    levels = ctx_count.bit_length() - 1
    block_index = block_index.T
    hbm = [pltpu.with_memory_space_constraint(each, pltpu.HBM) for each in (block_index, keys, values)]
    own, *sends = gather_blocks(*hbm, ctx_count, levels)
    blocks = [rotate(sends[level_num], "ctx", 2**level_num) for level_num in range(levels)]
    both, queries_t, grad_t, weights, grad_probs, stats = own_scores(queries, grad_out, own)
    scored = [block_scores(queries_t, grad_t, block) for block in blocks]
    sent, held, coef = partner_part(both, stats, scored)
    received = swap(sent, "head")
    part_kept, own_kept, own_sent, dq_local = own_part(both, own, blocks, weights, grad_probs, held, coef)
    own_received = swap(own_sent, "head")
    dq_gathered = spread(dq_local, head_count)
    parts = pair_parts(part_kept, received, levels)
    returned = []
    for level_num in range(levels):
        returned.append(rotate(parts[level_num], "ctx", -(2**level_num)))
    total = add_returned(block_index, own_kept, own_received, returned, ctx_count)
    gathered = spread(total, head_count)
    grad_queries = lay_queries(dq_gathered)
    grad_keys, grad_values = lay_keys(gathered)
    return (grad_queries, grad_keys, grad_values)


def solution(mesh):
    placed = (P("ctx", "head"), P("ctx", None), P("ctx", None), P("ctx", "head"), P())
    return jax.shard_map(
        on_device,
        mesh=mesh,
        in_specs=placed,
        out_specs=(P(("ctx", "head"), None), P(("ctx", "head"), None), P(("ctx", "head"), None)),
        check_vma=False,
    )
```

```python
import jax
import jax.numpy as jnp
from jax import lax
from jax.experimental import pallas as pl
from jax.experimental.pallas import tpu as pltpu
from jax.sharding import PartitionSpec as P


HD = 128
BLK = 256
NEG = -1e30
SCALE = HD**-0.5
FACTOR = SCALE * 1.4426950408889634
HBM = pl.BlockSpec(memory_space=pltpu.HBM)
VMEM = pl.BlockSpec(memory_space=pltpu.VMEM)
SMEM = pl.BlockSpec(memory_space=pltpu.SMEM)


def rotate(value, axis, steps):
    count = lax.axis_size(axis)
    return lax.ppermute(value, axis, [(source, (source + steps) % count) for source in range(count)])


def swap(value, axis):
    return lax.ppermute(value, axis, [(source, source ^ 1) for source in range(lax.axis_size(axis))])


def block_start(index_ref, ctx_index, level_num, ctx_count):
    target = jnp.minimum(ctx_index + 2**level_num, ctx_count - 1)
    return pl.multiple_of(index_ref[level_num, target] * BLK, BLK)


def gather_blocks(block_index, keys, values, ctx_count, levels):
    def body(index_hbm, key_ref, value_ref, own_ref, *refs):
        sends, index_ref, sems = refs[:levels], refs[levels], refs[levels + 1]
        begin = pl.multiple_of(lax.axis_index("head") // 2 * HD, HD)
        started = [pltpu.make_async_copy(index_hbm, index_ref, sems.at[2])]
        for half, source in ((0, key_ref), (1, value_ref)):
            started.append(
                pltpu.make_async_copy(
                    source.at[:, pl.ds(begin, HD)], own_ref.at[:, half * HD : (half + 1) * HD], sems.at[half]
                )
            )
        for copy in started:
            copy.start()
        for copy in started:
            copy.wait()
        ctx_index = lax.axis_index("ctx")
        for level_num in range(levels):
            start = block_start(index_ref, ctx_index, level_num, ctx_count)
            sends[level_num][...] = own_ref[pl.ds(start, BLK), :]

    return pl.pallas_call(
        body,
        out_shape=(jax.ShapeDtypeStruct((keys.shape[0], 2 * HD), keys.dtype),)
        + (jax.ShapeDtypeStruct((BLK, 2 * HD), keys.dtype),) * levels,
        in_specs=[HBM, HBM, HBM],
        out_specs=(VMEM,) * (levels + 1),
        scratch_shapes=[pltpu.SMEM(block_index.shape, jnp.int32), pltpu.SemaphoreType.DMA((3,))],
        compiler_params=params(4),
        name="gather_blocks",
    )(block_index, keys, values)


def dot(left, right):
    return jnp.dot(left, right, preferred_element_type=jnp.float32)


def spot(number):
    return slice(number * BLK, (number + 1) * BLK)


def params(mib):
    return pltpu.CompilerParams(vmem_limit_bytes=mib << 20)


def cost(dots, nbytes):
    return pl.CostEstimate(flops=dots * 2 * BLK * BLK * HD, bytes_accessed=nbytes, transcendentals=0)


def pairs(row_tiles):
    return [(part, number) for part in range(row_tiles) for number in range(part + 1)]


def score_tile(key_tile, value_tile, query_t, grad_t, seen=None):
    scores = dot(key_tile, query_t)
    if seen is not None:
        scores = jnp.where(seen, scores, NEG)
    top = jnp.max(scores, axis=0, keepdims=True) * FACTOR
    weights = jnp.exp2(scores * FACTOR - top)
    grad_probs = dot(value_tile, grad_t)
    total = jnp.sum(weights, axis=0, keepdims=True)
    product = jnp.sum(weights * grad_probs, axis=0, keepdims=True)
    return weights, grad_probs, (top, total, product)


def own_scores(queries, grad_out, own):
    rows, width = queries.shape
    row_tiles, heads = rows // BLK, width // HD
    places = pairs(row_tiles)
    total = heads * len(places)

    def body(q_ref, g_ref, own_ref, both_ref, qt_ref, gt_ref, weight_ref, prob_ref, stat_ref):
        both_ref[0], both_ref[1] = q_ref[...], g_ref[...]
        key_at = lax.broadcasted_iota(jnp.int32, (BLK, BLK), 0)
        causal = key_at <= lax.broadcasted_iota(jnp.int32, (BLK, BLK), 1)
        for head in range(heads):
            columns = slice(head * HD, (head + 1) * HD)
            for part in range(row_tiles):
                query_t, grad_t = q_ref[spot(part), columns].T, g_ref[spot(part), columns].T
                qt_ref[columns, spot(part)] = query_t
                gt_ref[columns, spot(part)] = grad_t
                for number in range(part + 1):
                    place = head * len(places) + places.index((part, number))
                    weight_ref[place], prob_ref[place], found = score_tile(
                        own_ref[spot(number), :HD],
                        own_ref[spot(number), HD:],
                        query_t,
                        grad_t,
                        causal if number == part else None,
                    )
                    at = head * row_tiles + part
                    for row, each in enumerate(found):
                        stat_ref[row, number, at : at + 1] = each
                for number in range(part + 1, row_tiles):
                    at = head * row_tiles + part
                    for row, each in enumerate((NEG, 0.0, 0.0)):
                        stat_ref[row, number, at : at + 1] = jnp.full((1, BLK), each, jnp.float32)

    tiles = jax.ShapeDtypeStruct((total, BLK, BLK), jnp.float32)
    turned = jax.ShapeDtypeStruct((width, rows), jnp.bfloat16)
    return pl.pallas_call(
        body,
        out_shape=(
            jax.ShapeDtypeStruct((2, rows, width), jnp.bfloat16),
            turned,
            turned,
            tiles,
            tiles,
            jax.ShapeDtypeStruct((3, row_tiles, heads * row_tiles, BLK), jnp.float32),
        ),
        in_specs=[VMEM] * 3,
        out_specs=(VMEM,) * 6,
        compiler_params=params(8),
        cost_estimate=cost(2 * total, 2 << 20),
        name="own_scores",
    )(queries, grad_out, own)


def block_scores(queries_t, grad_t, block):
    width, rows = queries_t.shape
    row_tiles, heads = rows // BLK, width // HD

    def body(qt_ref, gt_ref, block_ref, weight_ref, prob_ref, stat_ref):
        for head in range(heads):
            columns = slice(head * HD, (head + 1) * HD)
            for part in range(row_tiles):
                place = head * row_tiles + part
                weight_ref[place], prob_ref[place], found = score_tile(
                    block_ref[:, :HD], block_ref[:, HD:], qt_ref[columns, spot(part)], gt_ref[columns, spot(part)]
                )
                for row, each in enumerate(found):
                    stat_ref[row, place : place + 1] = each

    tiles = jax.ShapeDtypeStruct((heads * row_tiles, BLK, BLK), jnp.float32)
    return pl.pallas_call(
        body,
        out_shape=(tiles, tiles, jax.ShapeDtypeStruct((3, heads * row_tiles, BLK), jnp.float32)),
        in_specs=[VMEM] * 3,
        out_specs=(VMEM,) * 3,
        compiler_params=params(8),
        cost_estimate=cost(2 * heads * row_tiles, 2 << 20),
        name="block_scores",
    )(queries_t, grad_t, block)


def kinds():
    keep = lax.axis_index("head") % 2
    scales = [jnp.where(kind == 0, SCALE, 1.0) for kind in (keep, 1 - keep)]
    return keep, 1 - keep, scales[0], scales[1]


def partner_part(both, own_stats, scored):
    _, rows, width = both.shape
    levels, row_tiles, heads = len(scored), rows // BLK, width // HD

    def body(both_ref, own_ref, *refs):
        scored_refs = [refs[3 * level_num : 3 * level_num + 3] for level_num in range(levels)]
        send_ref, held_ref, coef_ref, chosen_ref = refs[3 * levels :]
        ctx_index = lax.axis_index("ctx")
        live = [ctx_index >= 2**level_num for level_num in range(levels)]
        stats = [[level_refs[2][row] for level_refs in scored_refs] for row in range(3)]
        tops = [jnp.where(live[level_num], stats[0][level_num], NEG) for level_num in range(levels)]
        tops += [own_ref[0, number] for number in range(row_tiles)]
        row_max = tops[0]
        for top in tops[1:]:
            row_max = jnp.maximum(row_max, top)
        ratios = [jnp.exp2(top - row_max) for top in tops]
        sums, products = (stats[row] + [own_ref[row, number] for number in range(row_tiles)] for row in (1, 2))
        inverse = 1.0 / sum(each * ratio for each, ratio in zip(sums, ratios))
        for number, ratio in enumerate(ratios):
            coef_ref[number] = ratio * inverse
        coef_ref[levels + row_tiles] = sum(each * ratio for each, ratio in zip(products, ratios)) * inverse
        _, send, _, scale = kinds()
        for level_num in range(levels):
            weight_ref, prob_ref, _ = scored_refs[level_num]
            sent = 0.0
            for head in range(heads):
                for part in range(row_tiles):
                    at = head * row_tiles + part
                    row = slice(at, at + 1)
                    probs = weight_ref[at] * coef_ref[level_num, row]
                    low = (probs * (prob_ref[at] - coef_ref[levels + row_tiles, row])).astype(jnp.bfloat16)
                    probs = probs.astype(jnp.bfloat16)
                    held_ref[0, head, spot(level_num), spot(part)] = low
                    held_ref[1, head, spot(level_num), spot(part)] = probs
                    chosen_ref[head, spot(level_num), spot(part)] = jnp.where(send == 0, low, probs)
                columns = slice(head * HD, (head + 1) * HD)
                sent += dot(chosen_ref[head, spot(level_num)], both_ref[send, :, columns])
            send_ref[spot(level_num)] = (sent * scale).astype(jnp.bfloat16)

    return pl.pallas_call(
        body,
        out_shape=(
            jax.ShapeDtypeStruct((levels * BLK, HD), jnp.bfloat16),
            jax.ShapeDtypeStruct((2, heads, levels * BLK, rows), jnp.bfloat16),
            jax.ShapeDtypeStruct((levels + row_tiles + 1, heads * row_tiles, BLK), jnp.float32),
        ),
        in_specs=[VMEM] * (2 + 3 * levels),
        out_specs=(VMEM,) * 3,
        scratch_shapes=[pltpu.VMEM((heads, levels * BLK, rows), jnp.bfloat16)],
        compiler_params=params(8),
        cost_estimate=cost(2 * heads * row_tiles * levels, 2 << 20),
        name="partner_part",
    )(both, own_stats, *[each for level in scored for each in level])


def own_part(both, own, blocks, weights, grad_probs, held, coef):
    _, rows, width = both.shape
    levels, row_tiles, heads = len(blocks), rows // BLK, width // HD
    places = pairs(row_tiles)
    total = heads * len(places)

    def body(both_ref, own_ref, weight_ref, prob_ref, held_ref, coef_ref, *refs):
        block_refs = refs[:levels]
        part_ref, keep_ref, send_ref, dq_ref, kt_ref, own_held_ref = refs[levels:]
        keep, send, keep_scale, send_scale = kinds()
        for level_num in range(levels):
            kept = 0.0
            for head in range(heads):
                columns = slice(head * HD, (head + 1) * HD)
                kept += dot(held_ref[keep, head, spot(level_num)], both_ref[keep, :, columns])
            part_ref[spot(level_num)] = kept * keep_scale
        for number in range(row_tiles):
            kt_ref[:, spot(number)] = own_ref[spot(number), :HD].T
        for level_num in range(levels):
            kt_ref[:, spot(row_tiles + level_num)] = block_refs[level_num][:, :HD].T
        for head in range(heads):
            columns = slice(head * HD, (head + 1) * HD)
            for part in range(row_tiles):
                at = head * row_tiles + part
                row = slice(at, at + 1)
                delta = coef_ref[levels + row_tiles, row]
                for number in range(part + 1):
                    place = head * len(places) + places.index((part, number))
                    probs = weight_ref[place] * coef_ref[levels + number, row]
                    low = (probs * (prob_ref[place] - delta)).astype(jnp.bfloat16)
                    own_held_ref[0, head, spot(number), spot(part)] = low
                    own_held_ref[1, head, spot(number), spot(part)] = probs.astype(jnp.bfloat16)
                dq_t = dot(kt_ref[:, rows:], held_ref[0, head, :, spot(part)])
                seen = slice(0, (part + 1) * BLK)
                dq_t += dot(kt_ref[:, seen], own_held_ref[0, head, seen, spot(part)])
                dq_ref[spot(part), columns] = (dq_t * SCALE).T.astype(jnp.bfloat16)
        for number in range(row_tiles):
            kept = sent = 0.0
            seeing = slice(number * BLK, rows)
            for head in range(heads):
                columns = slice(head * HD, (head + 1) * HD)
                kept += dot(own_held_ref[keep, head, spot(number), seeing], both_ref[keep, seeing, columns])
                sent += dot(own_held_ref[send, head, spot(number), seeing], both_ref[send, seeing, columns])
            keep_ref[spot(number)] = kept * keep_scale
            send_ref[spot(number)] = (sent * send_scale).astype(jnp.bfloat16)

    return pl.pallas_call(
        body,
        out_shape=(
            jax.ShapeDtypeStruct((levels * BLK, HD), jnp.float32),
            jax.ShapeDtypeStruct((rows, HD), jnp.float32),
            jax.ShapeDtypeStruct((rows, HD), jnp.bfloat16),
            jax.ShapeDtypeStruct((rows, width), jnp.bfloat16),
        ),
        in_specs=[VMEM] * (6 + levels),
        out_specs=(VMEM,) * 4,
        scratch_shapes=[
            pltpu.VMEM((HD, rows + levels * BLK), jnp.bfloat16),
            pltpu.VMEM((2, heads, rows, rows), jnp.bfloat16),
        ],
        compiler_params=params(14),
        cost_estimate=cost(3 * total + 2 * heads * row_tiles * levels, 2 << 20),
        name="own_part",
    )(both, own, weights, grad_probs, held, coef, *blocks)


def pair_parts(kept, received, levels):
    def body(kept_ref, received_ref, *part_refs):
        for level_num in range(levels):
            total = kept_ref[spot(level_num)] + received_ref[spot(level_num)].astype(jnp.float32)
            part_refs[level_num][...] = total.astype(jnp.bfloat16)

    return pl.pallas_call(
        body,
        out_shape=(jax.ShapeDtypeStruct((BLK, HD), jnp.bfloat16),) * levels,
        in_specs=[VMEM] * 2,
        out_specs=(VMEM,) * levels,
        compiler_params=params(6),
        name="pair_parts",
    )(kept, received)


def add_returned(block_index, kept, received, returned, ctx_count):
    levels = len(returned)

    def body(index_ref, kept_ref, received_ref, *refs):
        out_ref, total_ref = refs[levels:]
        ctx_index = lax.axis_index("ctx")
        total_ref[...] = kept_ref[...] + received_ref[...].astype(jnp.float32)
        for level_num in range(levels):
            start = block_start(index_ref, ctx_index, level_num, ctx_count)
            total_ref[pl.ds(start, BLK), :] += refs[level_num][...].astype(jnp.float32)
        out_ref[...] = total_ref[...].astype(jnp.bfloat16)

    return pl.pallas_call(
        body,
        out_shape=jax.ShapeDtypeStruct(kept.shape, jnp.bfloat16),
        in_specs=[SMEM] + [VMEM] * (levels + 2),
        out_specs=VMEM,
        scratch_shapes=[pltpu.VMEM(kept.shape, jnp.float32)],
        compiler_params=params(6),
        name="add_returned",
    )(block_index, kept, received, *returned)


def lay_queries(gathered):
    count, token_rows, width = gathered.shape

    def body(in_ref, out_ref):
        for number in range(count):
            out_ref[:, number * width : (number + 1) * width] = in_ref[number]

    return pl.pallas_call(
        body,
        out_shape=jax.ShapeDtypeStruct((token_rows, count * width), gathered.dtype),
        in_specs=[VMEM],
        out_specs=VMEM,
        compiler_params=params(6),
        name="lay_queries",
    )(gathered)


def lay_keys(gathered):
    count, token_rows, _ = gathered.shape

    def body(in_ref, key_ref, value_ref):
        for number in range(count):
            kind_ref = key_ref if number % 2 == 0 else value_ref
            group = number // 2
            kind_ref[:, group * HD : (group + 1) * HD] = in_ref[number]

    shape = jax.ShapeDtypeStruct((token_rows, count // 2 * HD), gathered.dtype)
    return pl.pallas_call(
        body,
        out_shape=(shape, shape),
        in_specs=[VMEM],
        out_specs=(VMEM,) * 2,
        compiler_params=params(6),
        name="lay_keys",
    )(gathered)


def spread(value, head_count):
    split = value.reshape(head_count, value.shape[0] // head_count, value.shape[1])
    return lax.all_to_all(split, "head", split_axis=0, concat_axis=0, tiled=True)


def on_device(queries, keys, values, grad_out, block_index):
    ctx_count = lax.axis_size("ctx")
    head_count = lax.axis_size("head")
    levels = ctx_count.bit_length() - 1
    block_index = block_index.T
    hbm = [pltpu.with_memory_space_constraint(each, pltpu.HBM) for each in (block_index, keys, values)]
    own, *sends = gather_blocks(*hbm, ctx_count, levels)
    blocks = [rotate(sends[level_num], "ctx", 2**level_num) for level_num in range(levels)]
    both, queries_t, grad_t, weights, grad_probs, stats = own_scores(queries, grad_out, own)
    scored = [block_scores(queries_t, grad_t, block) for block in blocks]
    sent, held, coef = partner_part(both, stats, scored)
    received = swap(sent, "head")
    part_kept, own_kept, own_sent, dq_local = own_part(both, own, blocks, weights, grad_probs, held, coef)
    own_received = swap(own_sent, "head")
    dq_gathered = spread(dq_local, head_count)
    parts = pair_parts(part_kept, received, levels)
    returned = []
    for level_num in range(levels):
        returned.append(rotate(parts[level_num], "ctx", -(2**level_num)))
    total = add_returned(block_index, own_kept, own_received, returned, ctx_count)
    gathered = spread(total, head_count)
    grad_queries = lay_queries(dq_gathered)
    grad_keys, grad_values = lay_keys(gathered)
    return (grad_queries, grad_keys, grad_values)


def solution(mesh):
    placed = (P("ctx", "head"), P("ctx", None), P("ctx", None), P("ctx", "head"), P())
    return jax.shard_map(
        on_device,
        mesh=mesh,
        in_specs=placed,
        out_specs=(P(("ctx", "head"), None), P(("ctx", "head"), None), P(("ctx", "head"), None)),
        check_vma=False,
    )
```
